256 devices in a mesh: row: 16 (over x, z_lo), col: 16 (over y, z_hi, core).
Axes of the slice: x: 4, y: 4, z: 8 (z_hi: 2, z_lo: 4; z = z_hi * 4 + z_lo), core: 2. Of those that a mesh axis runs over, the one named last changes fastest.
Arguments:
- potential: float32 [32, 64, 512], P('row', 'col'), may hold values from -6 to 6
- basis: bfloat16 [32, 64, 384, 512], P('row', 'col'), may hold values from -6 to 6
- hamiltonian: bfloat16 [6144, 6144], P('row', 'col'), may hold values from -0.078125 to 0.078125
- density: bfloat16 [2, 6144, 6144], P(None, 'row', 'col'), may hold values from -6 to 6
- hmask: int32 [48, 48], replicated, may hold values from 0 to 1, as said below
- pmask: int32 [48, 48], replicated, may hold values from 0 to 1, as said below
Outputs:
- propagated: bfloat16 [2, 6144, 6144], P(None, 'row', 'col')
The draws below stay inside these ranges and needn't reach their ends.
Inputs may be any that keep to these rules, and one draw needn't show every extreme that they name: hmask[I, I] is always 1; every other block is 1 with probability 1/2, independently. pmask follows the same law as hmask, drawn independently.
All inputs are finite; a program needn't handle non-finite values.
Results may differ from the reference program's by a relative error of at most 0.0062.
Values may be sent and summed in bfloat16 or wider, within the bound.
A program may use at most 64 MiB of HBM per device.

```python
import jax
import jax.numpy as jnp
from jax import lax

BLK = 128
KB = 3
CX = 2
GZ = 512
NBLK = 48
ORDER = 6144
GX = 32
GY = 64
N_ROW = 16


def random_pattern(key):
    index = jnp.arange(NBLK, dtype=jnp.int32)
    same = index[:, None] == index[None, :]
    coins = jax.random.randint(key, (NBLK, NBLK), 0, 2)
    keep = (coins > 0) | same
    return keep.astype(jnp.int32)


def draw_hmask(key, part):
    return random_pattern(jax.random.fold_in(key, 11))


def draw_pmask(key, part):
    return random_pattern(jax.random.fold_in(key, 23))


def levels(rng, dims, split, least, top_value):
    def one(position, shards_of):
        draws = jax.random.uniform(jax.random.fold_in(jax.random.fold_in(rng, 6), position), (shards_of,), jnp.float32, least / len(split), top_value / len(split))
        return jnp.repeat(jnp.exp(draws), dims[position] // shards_of).reshape((-1,) + (1,) * (len(dims) - position - 1))

    loudness = one(*split[0])
    for cut in split[1:]:
        loudness = loudness * one(*cut)
    return loudness


def gaussian(stream_key, extent, deviation, bound, pieces=(), held_as=jnp.bfloat16):
    result = deviation * jax.random.normal(stream_key, extent, jnp.float32)
    if pieces:
        result = result * levels(stream_key, extent, pieces, -0.22, 0.18)
    return jnp.clip(result, -bound, bound).astype(held_as)


def setup_inputs(seed: int = 0) -> dict:
    key_of = jax.random.split(jax.random.key(seed), 7)
    return {
        "potential": gaussian(key_of[0], (GX, GY, GZ), 1.0, 6.0, ((0, 16), (1, 16)), jnp.float32),
        "basis": gaussian(key_of[1], (GX, GY, KB * BLK, GZ), 1.0, 6.0, ((0, 16), (1, 16))),
        "hamiltonian": gaussian(key_of[2], (ORDER, ORDER), ORDER ** -0.5, 0.078125, ((0, 16), (1, 16))),
        "density": gaussian(key_of[3], (2, ORDER, ORDER), 1.0, 6.0, ((1, 16), (2, 16))),
        "hmask": draw_hmask(jax.random.fold_in(key_of[6], 71), 0),
        "pmask": draw_pmask(jax.random.fold_in(key_of[6], 71), 0),
    }


KAPPA = 0.4
TIME_STEP = 0.5


def screened(potential):
    padded = jnp.pad(potential, 1)
    beside = padded[2:, 1:-1, 1:-1] + padded[:-2, 1:-1, 1:-1]
    beside = beside + padded[1:-1, 2:, 1:-1] + padded[1:-1, :-2, 1:-1]
    beside = beside + padded[1:-1, 1:-1, 2:] + padded[1:-1, 1:-1, :-2]
    return potential + KAPPA * (beside - 6.0 * potential)


def integrate(packed):
    slab_values, table = packed
    weighted = (table.astype(jnp.float32) * slab_values[:, :, None, None, :]).astype(jnp.bfloat16)
    weighted = lax.optimization_barrier(weighted)
    return jnp.einsum("xykaz,xykbz->kab", weighted.astype(jnp.float32), table.astype(jnp.float32))


def reference(potential, basis, hamiltonian, density, hmask, pmask):
    effective = screened(potential)
    slab_v = effective.reshape(N_ROW, CX, GY, GZ)
    slab_b = basis.reshape(N_ROW, CX, GY, KB, BLK, GZ)
    blocks = lax.map(integrate, (slab_v, slab_b))
    factor = float(BLK * CX * GY * GZ) ** -0.5
    potential_blocks = (blocks * factor).reshape(NBLK, BLK, BLK).astype(jnp.bfloat16)
    masked_h = (hamiltonian.reshape(NBLK, BLK, NBLK, BLK) * hmask[:, None, :, None].astype(jnp.bfloat16)).reshape(ORDER, ORDER)
    pattern = pmask[None, :, None, :, None]
    masked_p = (density.reshape(2, NBLK, BLK, NBLK, BLK) * pattern.astype(jnp.bfloat16)).reshape(2, ORDER, ORDER)

    def apply(operand):
        remote = jnp.stack([jnp.dot(masked_h, operand[0], preferred_element_type=jnp.float32),
                            jnp.dot(masked_h, operand[1], preferred_element_type=jnp.float32)])
        diagonal_term = jnp.einsum("kab,skbc->skac", potential_blocks.astype(jnp.float32),
                                   operand.reshape(2, NBLK, BLK, ORDER).astype(jnp.float32))
        return remote + diagonal_term.reshape(2, ORDER, ORDER)

    first = apply(masked_p)
    first_rounded = first.astype(jnp.bfloat16)
    second = apply(first_rounded)
    base = masked_p.astype(jnp.float32)
    half_square = 0.5 * TIME_STEP * TIME_STEP
    real_part = base[0] + TIME_STEP * first[1] - half_square * second[0]
    imag_part = base[1] - TIME_STEP * first[0] - half_square * second[1]
    stacked = jnp.stack([real_part, imag_part]).reshape(2, NBLK, BLK, NBLK, BLK) * pattern.astype(jnp.float32)
    return stacked.reshape(2, ORDER, ORDER).astype(jnp.bfloat16)
```

```python
import functools
import heapq

import jax
import jax.numpy as jnp
from jax import lax
from jax.experimental import pallas as pl
from jax.experimental.pallas import tpu as pltpu
from jax.sharding import PartitionSpec as P

BLK = 128
KAPPA = 0.4
TIME_STEP = 0.5
MESH = pl.DeviceIdType.MESH

STEPS = 3
Y_FIRST = (16, 16, 32)
ROWS = 64
WIDE = 384


def plus_hops(s):
    return 4 if s % 2 == 0 else 3


def antipode_plus(dz):
    return dz % 2 == 0


def messages():
    out = {}
    for s in range(STEPS):
        a_kb, b_kb = Y_FIRST[s] * 1.5, (ROWS - Y_FIRST[s]) * 1.5
        out["Hm", s] = ("m", 48, [], ("H", s))
        up, down = plus_hops(s), 7 - plus_hops(s)
        for t in range(1, up + 1):
            out["bz+", s, t] = ("z+", b_kb, [("b", s, 0, 1 - t)], ("b", s, 0, -t))
        for t in range(1, down + 1):
            out["bz-", s, t] = ("z-", b_kb, [("b", s, 0, t - 1)], ("b", s, 0, t))
        for dz in range(-up, down + 1):
            out["by+", s, dz] = ("y+", b_kb, [("b", s, 0, dz)], ("b", s, -1, dz))
            out["by-", s, dz] = ("y-", b_kb, [("b", s, 0, dz)], ("b", s, 1, dz))
            if antipode_plus(dz):
                out["by2", s, dz] = ("y+", b_kb, [("b", s, -1, dz)], ("b", s, 2, dz))
            else:
                out["by2", s, dz] = ("y-", b_kb, [("b", s, 1, dz)], ("b", s, 2, dz))
        out["ay+", s] = ("y+", a_kb, [("a", s, 0)], ("a", s, -1))
        out["ay-", s] = ("y-", a_kb, [("a", s, 0)], ("a", s, 1))
        if s % 2 == 0:
            out["ay2", s] = ("y+", a_kb, [("a", s, -1)], ("a", s, 2))
        else:
            out["ay2", s] = ("y-", a_kb, [("a", s, 1)], ("a", s, 2))
        whole = [("a", s, 0), ("a", s, -1), ("a", s, 1), ("a", s, 2)]
        for t in range(1, up + 1):
            needs = whole if t == 1 else [("A4", s, 1 - t)]
            out["az+", s, t] = ("z+", 4 * a_kb, needs, ("A4", s, -t))
        for t in range(1, down + 1):
            needs = whole if t == 1 else [("A4", s, t - 1)]
            out["az-", s, t] = ("z-", 4 * a_kb, needs, ("A4", s, t))
    for rb in range(4):
        out["Px+", rb] = ("x+", 144, [("P", 0, rb)], ("P", -1, rb))
        out["Px-", rb] = ("x-", 144, [("P", 0, rb)], ("P", 1, rb))
        if rb < 2:
            out["Px2", rb] = ("x+", 144, [("P", -1, rb)], ("P", 2, rb))
        else:
            out["Px2", rb] = ("x-", 144, [("P", 1, rb)], ("P", 2, rb))
        for dx in (0, -1, 1, 2):
            out["Pm", dx, rb] = ("m", 144, [("P", dx, rb)], ("Pm", dx, rb))
    for s in range(STEPS):
        out["Fx+", s] = ("x+", 192, [("F", 0, s)], ("F", -1, s))
        out["Fx-", s] = ("x-", 192, [("F", 0, s)], ("F", 1, s))
        out["F2+", s] = ("x+", 96, [("F", -1, s)], ("F2", 0, s))
        out["F2-", s] = ("x-", 96, [("F", 1, s)], ("F2", 1, s))
        for dx in (0, -1, 1):
            out["Fm", dx, s] = ("m", 192, [("F", dx, s)], ("Fm", dx, s))
        for e in (0, 1):
            out["Fm2", e, s] = ("m", 96, [("F2", e, s)], ("Fm2", e, s))
    out["Dm",] = ("m", 96, [], ("Dm",))
    for j in range(1, 8):
        out["Dr", j] = ("z+" if j % 2 else "y+", 12, [("Dc",)], ("Dr", j))
    for j in range(1, 4):
        out["Dy", j] = ("y-", 12, [("Df",)], ("Dy", j))
    for j in range(1, 8):
        out["Dz", j] = ("z-", 48, [("Df",)] + [("Dy", i) for i in (1, 2, 3)], ("Dz", j))
    return out


def tasks():
    out = {}
    for s in range(STEPS):
        out["Hready", s] = (0.05, [("H", s)], [("b", s, 0, 0), ("a", s, 0)])
    every_p = [("P", dx, rb) for dx in (0, -1, 1, 2) for rb in range(4)]
    every_p += [("Pm", dx, rb) for dx in (0, -1, 1, 2) for rb in range(4)]
    every_d = [("Dy", i) for i in (1, 2, 3)] + [("Dz", i) for i in range(1, 8)] + [("Df",)]
    for s in range(STEPS):
        up, down = plus_hops(s), 7 - plus_hops(s)
        near = [("b", s, dy, dz) for dy in (0, -1, 1) for dz in range(-up, down + 1)]
        near += [("A4", s, dz) for dz in range(-up, down + 1) if dz] + [("a", s, 2)]
        far = [("b", s, 2, dz) for dz in range(-up, down + 1)]
        out["C1", s] = (3.2, near + far + every_p, [("C1", s)])
        out["Ff", s] = (0.5, [("C1", s)] + every_d, [("F", 0, s)])
    out["Dc",] = (0.2, [("Dm",)], [("Dc",)])
    out["Df",] = (0.2, [("Dc",)] + [("Dr", j) for j in range(1, 8)], [("Df",)])
    all_a = [("C1", s) for s in range(STEPS)]
    for s in range(STEPS):
        out["S", s, 0] = (0.9, all_a + [("F", 0, s), ("Fm", 0, s)], [("S", s, 0)])
        out["S", s, -1] = (0.8, all_a + [("F", -1, s), ("Fm", -1, s)], [("S", s, -1)])
        out["S", s, 1] = (0.8, all_a + [("F", 1, s), ("Fm", 1, s)], [("S", s, 1)])
        far = [("F2", e, s) for e in (0, 1)] + [("Fm2", e, s) for e in (0, 1)]
        out["S", s, 2] = (0.8, all_a + far, [("S", s, 2)])
    return out


RATE = {"m": 200.0}
LINK_RATE = 42.0
BACKLOG = 4.0


def rank_of(name):
    kind = name[0]
    if kind in ("Hm", "Dm", "Dr", "Dy", "Dz"):
        return (-1, 0)
    if kind[0] in "PF":
        return (0, 0)
    return (name[1], 0 if kind in ("bz+", "bz-", "ay+", "ay-", "ay2") else 1)


def schedule():
    every, work = messages(), tasks()
    given_by = {m[3]: n for n, m in every.items()}
    have, sent, done = set(), set(), set()
    free = {}
    arrivals = []
    order = []
    now = 0.0
    free["z+"] = free["z-"] = 2 * 144 / LINK_RATE / 1.0
    for rb in range(4):
        heapq.heappush(arrivals, (16.0 + rb, 0, ("P0", rb)))
    count = 0

    def issue():
        nonlocal count
        ready = [n for n, m in every.items() if n not in sent and all(d in have for d in m[2])]
        ready.sort(key=rank_of)
        for name in ready:
            link, size, _, _ = every[name]
            start = max(now, free.get(link, 0.0))
            if start - now > BACKLOG and link != "m":
                continue
            end = start + size / RATE.get(link, LINK_RATE)
            free[link] = end
            sent.add(name)
            count += 1
            heapq.heappush(arrivals, (end + (1.0 if link == "m" else 1.8), count, name))
            order.append(("send", name))

    while len(done) < len(work) or arrivals:
        issue()
        if arrivals and arrivals[0][0] <= now:
            _, _, name = heapq.heappop(arrivals)
            order.append(("wait", name))
            have.add(("P", 0, name[1]) if name[0] == "P0" else every[name][3])
            continue
        ready = [n for n, w in work.items() if n not in done and all(d in have for d in w[1])]
        if ready:
            name = ready[0]
            now += work[name][0]
            done.add(name)
            have.update(work[name][2])
            order.append(("work", name))
            continue
        later = [arrivals[0][0]] if arrivals else []
        waiting = [n for n, m in every.items() if n not in sent and all(d in have for d in m[2])]
        later += [free[every[n][0]] - BACKLOG + 0.01 for n in waiting]
        now = max(now + 0.01, min(later))
    return order, now


def core_kernel(order, h_ref, p_ref, part_ref, out_ref, a_buf, b_buf, f_buf, o_buf,
                f_acc, s_acc, d_mate, d_chip, d_all, d_got, d_fin,
                send_sem, recv_sem, local_sem, pin_sem, pin_send, ret_sem, ret_send):
    row, col = lax.axis_index("row"), lax.axis_index("col")
    x, zl = row // 4, row % 4
    y, zh, c = col // 4, (col // 2) % 2, col % 2
    z = zh * 4 + zl
    half = c

    def dev(dx=0, dy=0, dz=0, core=None):
        zz = (z + dz) % 8
        core = c if core is None else core
        return (((x + dx) % 4) * 4 + zz % 4, ((y + dy) % 4) * 4 + (zz // 4) * 2 + core)

    def dev_line(q, core):
        return (x * 4 + q, y * 4 + zh * 2 + core)

    barrier = pltpu.get_barrier_semaphore()
    friends = [dev(core=1 - c), dev(dx=1), dev(dx=-1)]
    friends += [dev(dy=j) for j in (1, 2, 3)] + [dev(dz=j) for j in range(1, 8)]
    friends += [dev(dy=j, dz=4) for j in (1, 2, 3)]
    friends += [dev_line((zl + j) % 4, 1 - c) for j in (1, 2, 3)]
    for friend in friends:
        pl.semaphore_signal(barrier, inc=1, device_id=friend, device_id_type=MESH)
    pl.semaphore_wait(barrier, len(friends))

    names = list(messages())
    index = {n: i for i, n in enumerate(names)}

    def block(s, dy, dz, color):
        zz = (z + dz) % 8
        rows = pl.ds(0, Y_FIRST[s]) if color == "a" else pl.ds(Y_FIRST[s], ROWS - Y_FIRST[s])
        return a_buf.at[s, (y + dy) % 4, zz // 4, zz % 4, rows]

    def block4(s, dz):
        zz = (z + dz) % 8
        return a_buf.at[s, :, zz // 4, zz % 4, pl.ds(0, Y_FIRST[s])]

    def lanes(core):
        return pl.ds(pl.multiple_of(core * WIDE, 128), WIDE)

    def b_slot(dx, rb, core):
        return b_buf.at[(x + dx) % 4, rb, :, core]

    def f_slot(dx, s, core, rbs):
        return f_buf.at[(x + dx) % 4, rbs, s, core]

    FULL, LOW, HIGH = pl.ds(0, 4), pl.ds(0, 2), pl.ds(2, 2)

    def ends(name):
        kind = name[0]
        if kind == "Hm":
            s = name[1]
            return (h_ref.at[s, 1 - c], a_buf.at[s, y, zh, zl, :, lanes(c)],
                    a_buf.at[s, y, zh, zl, :, lanes(1 - c)], dev(core=1 - c))
        if kind == "bz+":
            _, s, t = name
            src = block(s, 0, 1 - t, "b")
            return src, src, block(s, 0, -t, "b"), dev(dz=1)
        if kind == "bz-":
            _, s, t = name
            src = block(s, 0, t - 1, "b")
            return src, src, block(s, 0, t, "b"), dev(dz=-1)
        if kind == "by+":
            _, s, dz = name
            src = block(s, 0, dz, "b")
            return src, src, block(s, -1, dz, "b"), dev(dy=1)
        if kind == "by-":
            _, s, dz = name
            src = block(s, 0, dz, "b")
            return src, src, block(s, 1, dz, "b"), dev(dy=-1)
        if kind == "by2":
            _, s, dz = name
            way = 1 if antipode_plus(dz) else -1
            src = block(s, -way, dz, "b")
            return src, src, block(s, 2, dz, "b"), dev(dy=way)
        if kind == "ay+":
            src = block(name[1], 0, 0, "a")
            return src, src, block(name[1], -1, 0, "a"), dev(dy=1)
        if kind == "ay-":
            src = block(name[1], 0, 0, "a")
            return src, src, block(name[1], 1, 0, "a"), dev(dy=-1)
        if kind == "ay2":
            way = 1 if name[1] % 2 == 0 else -1
            src = block(name[1], -way, 0, "a")
            return src, src, block(name[1], 2, 0, "a"), dev(dy=way)
        if kind == "az+":
            _, s, t = name
            src = block4(s, 1 - t)
            return src, src, block4(s, -t), dev(dz=1)
        if kind == "az-":
            _, s, t = name
            src = block4(s, t - 1)
            return src, src, block4(s, t), dev(dz=-1)
        if kind == "Px+":
            src = b_slot(0, name[1], c)
            return src, src, b_slot(-1, name[1], c), dev(dx=1)
        if kind == "Px-":
            src = b_slot(0, name[1], c)
            return src, src, b_slot(1, name[1], c), dev(dx=-1)
        if kind == "Px2":
            way = 1 if name[1] < 2 else -1
            src = b_slot(-way, name[1], c)
            return src, src, b_slot(2, name[1], c), dev(dx=way)
        if kind == "Pm":
            _, dx, rb = name
            src = b_slot(dx, rb, c)
            return src, src, b_slot(dx, rb, 1 - c), dev(core=1 - c)
        if kind == "Fx+":
            src = f_slot(0, name[1], c, FULL)
            return src, src, f_slot(-1, name[1], c, FULL), dev(dx=1)
        if kind == "Fx-":
            src = f_slot(0, name[1], c, FULL)
            return src, src, f_slot(1, name[1], c, FULL), dev(dx=-1)
        if kind == "F2+":
            src = f_slot(-1, name[1], c, LOW)
            return src, src, f_slot(2, name[1], c, LOW), dev(dx=1)
        if kind == "F2-":
            src = f_slot(1, name[1], c, HIGH)
            return src, src, f_slot(2, name[1], c, HIGH), dev(dx=-1)
        if kind == "Fm":
            _, dx, s = name
            src = f_slot(dx, s, c, FULL)
            return src, src, f_slot(dx, s, 1 - c, FULL), dev(core=1 - c)
        if kind == "Fm2":
            _, e, s = name
            rbs = HIGH if e else LOW
            src = f_slot(2, s, c, rbs)
            return src, src, f_slot(2, s, 1 - c, rbs), dev(core=1 - c)
        if kind == "Dm":
            return part_ref.at[:, 1 - c], d_mate, d_mate, dev(core=1 - c)
        if kind == "Dr":
            j = name[1]
            dy, dz = j // 2, 4 * (j % 2)
            to = ((y + dy) % 4) * 2 + (zh + j % 2) % 2
            return d_chip.at[to], d_got.at[j - 1], d_got.at[j - 1], dev(dy=dy, dz=dz)
        if kind == "Dy":
            j = name[1]
            return d_fin, d_all.at[zl, y, zh], d_all.at[zl, (y - j) % 4, zh], dev(dy=j)
        if kind == "Dz":
            j = name[1]
            zz = (z - j) % 8
            src = d_all.at[zl, :, zh]
            return src, src, d_all.at[zz % 4, :, zz // 4], dev(dz=j)
        raise KeyError(name)

    def outgoing(name):
        src, dst, _, target = ends(name)
        i = index[name]
        return pltpu.make_async_remote_copy(
            src_ref=src, dst_ref=dst, send_sem=send_sem.at[i], recv_sem=recv_sem.at[i],
            device_id=target, device_id_type=MESH)

    def incoming(name):
        src, _, land, target = ends(name)
        i = index[name]
        return pltpu.make_async_remote_copy(
            src_ref=land, dst_ref=land, send_sem=send_sem.at[i], recv_sem=recv_sem.at[i],
            device_id=target, device_id_type=MESH)

    own = [pltpu.make_async_copy(h_ref.at[s, c], a_buf.at[s, y, zh, zl, :, lanes(c)],
                                 local_sem.at[s]) for s in range(STEPS)]
    for copy in own:
        copy.start()

    def p_copy(hf, r):
        q = 2 * c + hf
        src = p_ref.at[hf, :, r]
        here = (q == zl) & (r == c)
        dst = b_buf.at[x, zl, :, r]

        def local():
            return pltpu.make_async_copy(src, dst, pin_sem.at[zl])

        def remote():
            return pltpu.make_async_remote_copy(
                src_ref=src, dst_ref=dst, send_sem=pin_send.at[hf, r], recv_sem=pin_sem.at[zl],
                device_id=dev_line(q, r), device_id_type=MESH)

        return here, local, remote

    def start_p():
        for hf in range(2):
            for r in range(2):
                here, local, remote = p_copy(hf, r)

                @pl.when(here)
                def _():
                    local().start()

                @pl.when(jnp.logical_not(here))
                def _():
                    remote().start()

    def chunk_a(s, yy, zz):
        return a_buf[s, yy, zz].reshape(4 * ROWS, 2 * WIDE)

    def first_product(s):
        f_acc[s] = jnp.zeros((4 * ROWS, WIDE), jnp.float32)

        def body(k, carry):
            yy, zz = k // 2, k % 2
            right = b_buf[yy, pl.ds(zz * 2, 2)].reshape(2 * WIDE, WIDE)
            f_acc[s] += jnp.dot(chunk_a(s, yy, zz), right, preferred_element_type=jnp.float32)
            return carry

        lax.fori_loop(0, 8, body, 0)

    def diagonal(rb, s):
        return d_all[rb].reshape(STEPS, ROWS, BLK)[s].astype(jnp.bfloat16)

    def first_finish(s):
        for rb in range(4):
            rows = pl.ds(rb * ROWS, ROWS)
            right = b_buf[x, rb, s].reshape(BLK, WIDE)
            total = f_acc[s, rows] + jnp.dot(diagonal(rb, s), right,
                                             preferred_element_type=jnp.float32)
            f_acc[s, rows] = total
            f_buf[x, rb, s, c] = total.astype(jnp.bfloat16)

    def second_product(s, dx):
        xx = (x + dx) % 4
        tile = slice(s * BLK, (s + 1) * BLK), slice(WIDE + s * BLK, WIDE + (s + 1) * BLK)

        def body(k, carry):
            t, zz = k // 2, k % 2
            left = jnp.concatenate(
                [a_buf[t, xx, zz, :, :, cut].reshape(4 * ROWS, BLK) for cut in tile], axis=1)
            right = jnp.concatenate(
                [f_buf[xx, zz * 2 + e, s].reshape(BLK, WIDE) for e in range(2)], axis=0)
            s_acc[t] += jnp.dot(left, right, preferred_element_type=jnp.float32)
            return carry

        lax.fori_loop(0, 6, body, 0)
        if dx == 0:
            for rb in range(4):
                rows = pl.ds(rb * ROWS, ROWS)
                right = f_buf[x, rb, s].reshape(BLK, WIDE)
                s_acc[s, rows] += jnp.dot(diagonal(rb, s), right,
                                          preferred_element_type=jnp.float32)

    def finish_integrals():
        mine = y * 2 + zh
        total = d_chip[mine]
        for j in range(7):
            total = total + d_got[j]
        factor = float(BLK * 2 * 64 * 512) ** -0.5
        d_fin[...] = total * factor
        d_all[zl, y, zh] = total * factor

    def run(name):
        kind = name[0]
        if kind == "Hready":
            own[name[1]].wait()
        elif kind == "C1":
            first_product(name[1])
        elif kind == "Ff":
            first_finish(name[1])
        elif kind == "S":
            second_product(name[1], name[2])
        elif kind == "Dc":
            d_chip[...] = (part_ref[:, c] + d_mate[...]).reshape(8, 24, BLK)
        elif kind == "Df":
            finish_integrals()

    start_p()
    s_acc[...] = jnp.zeros_like(s_acc)
    for what, name in order:
        if what == "send":
            outgoing(name).start()
        elif what == "wait":
            if name[0] == "P0":
                rb = name[1]
                land = b_buf.at[x, rb, :, c]
                pltpu.make_async_copy(land, land, pin_sem.at[rb]).wait()
            else:
                incoming(name).wait_recv()
        else:
            run(name)

    lane = lax.broadcasted_iota(jnp.int32, (ROWS, BLK), 1)
    quarter = 0.5 * TIME_STEP * TIME_STEP

    def back(rb):
        here = (rb == zl) & (zl // 2 == c)
        src = o_buf.at[rb]
        dst = out_ref.at[zl % 2, :, c]

        def local():
            return pltpu.make_async_copy(src, dst, ret_sem.at[zl % 2, c])

        def remote():
            return pltpu.make_async_remote_copy(
                src_ref=src, dst_ref=dst, send_sem=ret_send.at[rb],
                recv_sem=ret_sem.at[zl % 2, c],
                device_id=dev_line(rb, zl // 2), device_id_type=MESH)

        return here, local, remote

    for rb in range(4):
        rows = pl.ds(rb * ROWS, ROWS)
        for s in range(STEPS):
            base = b_buf[x, rb, s, c].astype(jnp.float32)
            f = f_acc[s, rows]
            mixed = f[:, 2 * BLK:]
            turned = pltpu.roll(mixed, BLK // 2, 1)
            turn = jnp.concatenate(
                [f[:, BLK:2 * BLK], -f[:, :BLK], jnp.where(lane < BLK // 2, turned, -turned)],
                axis=1)
            o_buf[rb, s] = (base + TIME_STEP * turn - quarter * s_acc[s, rows]).astype(jnp.bfloat16)
        here, local, remote = back(rb)

        @pl.when(here)
        def _():
            local().start()

        @pl.when(jnp.logical_not(here))
        def _():
            remote().start()

    for hf in range(2):
        for r in range(2):
            land = out_ref.at[hf, :, r]
            pltpu.make_async_copy(land, land, ret_sem.at[hf, r]).wait()

    for what, name in order:
        if what == "send":
            outgoing(name).wait_send()
    for hf in range(2):
        for r in range(2):
            here, _, remote = p_copy(hf, r)

            @pl.when(jnp.logical_not(here))
            def _():
                remote().wait_send()
    for rb in range(4):
        here, _, remote = back(rb)

        @pl.when(jnp.logical_not(here))
        def _():
            remote().wait_send()


def propagate(h, p, part):
    order, _ = schedule()
    total = len(messages())
    bf, f32 = jnp.bfloat16, jnp.float32
    any_space = pl.BlockSpec(memory_space=pl.ANY)
    vmem = pl.BlockSpec(memory_space=pltpu.VMEM)
    return pl.pallas_call(
        functools.partial(core_kernel, order),
        out_shape=jax.ShapeDtypeStruct((2, STEPS, 2, ROWS, WIDE), bf),
        in_specs=[any_space, any_space, vmem],
        out_specs=any_space,
        scratch_shapes=[
            pltpu.VMEM((STEPS, 4, 2, 4, ROWS, 2 * WIDE), bf),
            pltpu.VMEM((4, 4, STEPS, 2, ROWS, WIDE), bf),
            pltpu.VMEM((4, 4, STEPS, 2, ROWS, WIDE), bf),
            pltpu.VMEM((4, STEPS, ROWS, WIDE), bf),
            pltpu.VMEM((STEPS, 4 * ROWS, WIDE), f32),
            pltpu.VMEM((STEPS, 4 * ROWS, WIDE), f32),
            pltpu.VMEM((STEPS, ROWS, BLK), f32),
            pltpu.VMEM((8, 24, BLK), f32),
            pltpu.VMEM((4, 4, 2, 24, BLK), f32),
            pltpu.VMEM((7, 24, BLK), f32),
            pltpu.VMEM((24, BLK), f32),
            pltpu.SemaphoreType.DMA((total,)),
            pltpu.SemaphoreType.DMA((total,)),
            pltpu.SemaphoreType.DMA((STEPS,)),
            pltpu.SemaphoreType.DMA((4,)),
            pltpu.SemaphoreType.DMA((2, 2)),
            pltpu.SemaphoreType.DMA((2, 2)),
            pltpu.SemaphoreType.DMA((4,)),
        ],
        compiler_params=pltpu.CompilerParams(
            collective_id=0, has_side_effects=True, vmem_limit_bytes=48 << 20),
        name="propagate",
    )(h, p, part)


def extended_2(block, sides, width):
    for axis, dim in sides:
        count = lax.axis_size(axis)
        forward = [(i, i + 1) for i in range(count - 1)]
        backward = [(target, source) for source, target in forward]
        low = lax.ppermute(
            lax.slice_in_dim(block, block.shape[dim] - width, None, axis=dim), axis, forward
        )
        high = lax.ppermute(lax.slice_in_dim(block, 0, width, axis=dim), axis, backward)
        block = jnp.concatenate([low, block, high], axis=dim)
    return block


def partial_integrals(potential, basis):
    width_x, width_y, depth_z = potential.shape
    extended = extended_2(potential, (("row", 0), ("col", 1)), 1)
    padded = jnp.pad(extended, ((0, 0), (0, 0), (1, 1)))
    beside = padded[2:, 1:-1, 1:-1] + padded[:-2, 1:-1, 1:-1]
    beside = beside + padded[1:-1, 2:, 1:-1] + padded[1:-1, :-2, 1:-1]
    beside = beside + padded[1:-1, 1:-1, 2:] + padded[1:-1, 1:-1, :-2]
    effective = potential + KAPPA * (beside - 6.0 * potential)
    blocks_here = basis.shape[2] // BLK
    weighted = (basis * effective[:, :, None, :]).astype(jnp.bfloat16)
    return jnp.einsum(
        "xykaz,xykbz->kab",
        weighted.reshape(width_x, width_y, blocks_here, BLK, depth_z),
        basis.reshape(width_x, width_y, blocks_here, BLK, depth_z),
        preferred_element_type=jnp.float32,
    )


def shards(potential, basis, hamiltonian, density, hmask, pmask):
    part = partial_integrals(potential, basis).reshape(STEPS, 2, ROWS, BLK)
    row_start = lax.axis_index("row") * 3
    col_start = lax.axis_index("col") * 3
    hpattern = lax.dynamic_slice(hmask, (row_start, col_start), (3, 3))
    ppattern = lax.dynamic_slice(pmask, (row_start, col_start), (3, 3))
    masked_h = (
        hamiltonian.reshape(3, BLK, 3, BLK) * hpattern[:, None, :, None].astype(jnp.bfloat16)
    ).reshape(STEPS, 2, ROWS, WIDE)
    masked_p = (
        density.reshape(2, 3, BLK, 3, BLK) * ppattern[None, :, None, :, None].astype(jnp.bfloat16)
    ).reshape(2, WIDE, WIDE)
    units = jnp.stack([
        jnp.concatenate(
            [masked_p[0, :, t * BLK:(t + 1) * BLK], masked_p[1, :, t * BLK:(t + 1) * BLK],
             masked_p[0, :, 256 + 64 * t:320 + 64 * t], masked_p[1, :, 256 + 64 * t:320 + 64 * t]],
            axis=1)
        for t in range(2)
    ]).reshape(2, STEPS, 2, ROWS, WIDE)
    result = propagate(masked_h, units, part).reshape(2, WIDE, WIDE)
    whole = jnp.stack([
        jnp.concatenate(
            [result[0, :, t * BLK:(t + 1) * BLK], result[1, :, t * BLK:(t + 1) * BLK],
             result[0, :, 256 + 64 * t:320 + 64 * t], result[1, :, 256 + 64 * t:320 + 64 * t]],
            axis=1)
        for t in range(2)
    ])
    whole = whole.reshape(2, 3, BLK, 3, BLK) * ppattern[None, :, None, :, None].astype(jnp.bfloat16)
    return whole.reshape(2, WIDE, WIDE)


def solution(mesh):
    in_specs = (
        P("row", "col", None),
        P("row", "col", None, None),
        P("row", "col"),
        P(None, "row", "col"),
        P(),
        P(),
    )
    out_specs = P(None, "row", "col")
    return jax.shard_map(shards, mesh=mesh, in_specs=in_specs, out_specs=out_specs, check_vma=False)
```

```python
import functools
import heapq

import jax
import jax.numpy as jnp
from jax import lax
from jax.experimental import pallas as pl
from jax.experimental.pallas import tpu as pltpu
from jax.sharding import PartitionSpec as P

BLK = 128
KAPPA = 0.4
TIME_STEP = 0.5
MESH = pl.DeviceIdType.MESH

STEPS = 3
Y_FIRST = (32, 16, 16)
ROWS = 64
WIDE = 384


def plus_hops(s):
    return 4 if s % 2 == 0 else 3


def antipode_plus(dz):
    return dz % 2 == 0


def messages():
    out = {}
    for s in range(STEPS):
        a_kb, b_kb = Y_FIRST[s] * 1.5, (ROWS - Y_FIRST[s]) * 1.5
        out["Hm", s] = ("m", 48, [], ("H", s))
        up, down = plus_hops(s), 7 - plus_hops(s)
        for t in range(1, up + 1):
            out["bz+", s, t] = ("z+", b_kb, [("b", s, 0, 1 - t)], ("b", s, 0, -t))
        for t in range(1, down + 1):
            out["bz-", s, t] = ("z-", b_kb, [("b", s, 0, t - 1)], ("b", s, 0, t))
        for dz in range(-up, down + 1):
            out["by+", s, dz] = ("y+", b_kb, [("b", s, 0, dz)], ("b", s, -1, dz))
            out["by-", s, dz] = ("y-", b_kb, [("b", s, 0, dz)], ("b", s, 1, dz))
            if antipode_plus(dz):
                out["by2", s, dz] = ("y+", b_kb, [("b", s, -1, dz)], ("b", s, 2, dz))
            else:
                out["by2", s, dz] = ("y-", b_kb, [("b", s, 1, dz)], ("b", s, 2, dz))
        out["ay+", s] = ("y+", a_kb, [("a", s, 0)], ("a", s, -1))
        out["ay-", s] = ("y-", a_kb, [("a", s, 0)], ("a", s, 1))
        if s % 2 == 0:
            out["ay2", s] = ("y+", a_kb, [("a", s, -1)], ("a", s, 2))
        else:
            out["ay2", s] = ("y-", a_kb, [("a", s, 1)], ("a", s, 2))
        whole = [("a", s, 0), ("a", s, -1), ("a", s, 1), ("a", s, 2)]
        for t in range(1, up + 1):
            needs = whole if t == 1 else [("A4", s, 1 - t)]
            out["az+", s, t] = ("z+", 4 * a_kb, needs, ("A4", s, -t))
        for t in range(1, down + 1):
            needs = whole if t == 1 else [("A4", s, t - 1)]
            out["az-", s, t] = ("z-", 4 * a_kb, needs, ("A4", s, t))
    for rb in range(4):
        out["Px+", rb] = ("x+", 144, [("P", 0, rb)], ("P", -1, rb))
        out["Px-", rb] = ("x-", 144, [("P", 0, rb)], ("P", 1, rb))
        if rb < 2:
            out["Px2", rb] = ("x+", 144, [("P", -1, rb)], ("P", 2, rb))
        else:
            out["Px2", rb] = ("x-", 144, [("P", 1, rb)], ("P", 2, rb))
        for dx in (0, -1, 1, 2):
            out["Pm", dx, rb] = ("m", 144, [("P", dx, rb)], ("Pm", dx, rb))
    for s in range(STEPS):
        for e in (0, 1):
            out["Fx+", s, e] = ("x+", 96, [("F", 0, s)], ("F", -1, s, e))
            out["Fx-", s, 1 - e] = ("x-", 96, [("F", 0, s)], ("F", 1, s, 1 - e))
        out["F2+", s] = ("x+", 96, [("F", -1, s, 0)], ("F", 2, s, 0))
        out["F2-", s] = ("x-", 96, [("F", 1, s, 1)], ("F", 2, s, 1))
        out["Fm", 0, s] = ("m", 192, [("F", 0, s)], ("Fm", 0, s))
        for dx in (-1, 1, 2):
            for e in (0, 1):
                out["Fm", dx, s, e] = ("m", 96, [("F", dx, s, e)], ("Fm", dx, s, e))
    out["Dm",] = ("m", 96, [("I", i) for i in range(4)], ("Dm",))
    for j in range(1, 8):
        out["Dr", j] = ("z+" if j % 2 else "y+", 12, [("Dc",)], ("Dr", j))
    for j in range(1, 4):
        out["Dy", j] = ("y-", 12, [("Df",)], ("Dy", j))
    for j in range(1, 8):
        out["Dz", j] = ("z-", 48, [("Df",)] + [("Dy", i) for i in (1, 2, 3)], ("Dz", j))
    return out


def tasks():
    out = {}
    for s in range(STEPS):
        out["Hready", s] = (0.05, [("H", s)], [("b", s, 0, 0), ("a", s, 0)])
    every_p = [("P", dx, rb) for dx in (0, -1, 1, 2) for rb in range(4)]
    every_p += [("Pm", dx, rb) for dx in (0, -1, 1, 2) for rb in range(4)]
    every_d = [("Dy", i) for i in (1, 2, 3)] + [("Dz", i) for i in range(1, 8)] + [("Df",)]
    for s in range(STEPS):
        up, down = plus_hops(s), 7 - plus_hops(s)
        near = [("b", s, dy, dz) for dy in (0, -1, 1) for dz in range(-up, down + 1)]
        near += [("A4", s, dz) for dz in range(-up, down + 1) if dz] + [("a", s, 2)]
        far = [("b", s, 2, dz) for dz in range(-up, down + 1)]
        out["C1", s, 0] = (2.4, near + every_p, [("C1", s, 0)])
        out["C1", s, 1] = (0.8, far + [("C1", s, 0)], [("C1", s, 1)])
        out["Ff", s] = (0.5, [("C1", s, 1)] + every_d, [("F", 0, s)])
    out["E",] = (0.5, [("halo",)], [("E",)])
    for i in range(4):
        out["I", i] = (1.5, [("E",)], [("I", i)])
    out["Dc",] = (0.2, [("Dm",)], [("Dc",)])
    out["Df",] = (0.2, [("Dc",)] + [("Dr", j) for j in range(1, 8)], [("Df",)])
    all_a = [("C1", s, 1) for s in range(STEPS)]
    for s in range(STEPS):
        out["S", s, 0] = (0.9, all_a + [("F", 0, s), ("Fm", 0, s)], [("S", s, 0)])
        for dx in (-1, 1, 2):
            needs = [(k, dx, s, e) for k in ("F", "Fm") for e in (0, 1)]
            out["S", s, dx] = (0.8, all_a + needs, [("S", s, dx)])
    return out


RATE = {"m": 200.0}
LINK_RATE = 42.0
BACKLOG = 4.0


def rank_of(name):
    kind = name[0]
    if kind in ("Hm", "Dm", "Dr", "Dy", "Dz"):
        return (-1, 0)
    if kind[0] in "PF":
        return (0, 0)
    return (name[1], 0 if kind in ("bz+", "bz-", "ay+", "ay-", "ay2") else 1)


def schedule():
    every, work = messages(), tasks()
    given_by = {m[3]: n for n, m in every.items()}
    have, sent, done = set(), set(), set()
    free = {}
    arrivals = []
    order = []
    now = 0.0
    free["z+"] = free["z-"] = 2 * 144 / LINK_RATE
    for rb in range(4):
        heapq.heappush(arrivals, (20.0 + rb, 0, ("P0", rb)))
    heapq.heappush(arrivals, (4.0, 0, ("halo",)))
    count = 0

    def issue():
        nonlocal count
        ready = [n for n, m in every.items() if n not in sent and all(d in have for d in m[2])]
        ready.sort(key=rank_of)
        for name in ready:
            link, size, _, _ = every[name]
            start = max(now, free.get(link, 0.0))
            if start - now > BACKLOG and link != "m":
                continue
            end = start + size / RATE.get(link, LINK_RATE)
            free[link] = end
            sent.add(name)
            count += 1
            wait = 6.0 if name[0] in ("Dr", "Dy", "Dz") else 1.0 if link == "m" else 1.8
            heapq.heappush(arrivals, (end + wait, count, name))
            order.append(("send", name))

    while len(done) < len(work) or arrivals:
        issue()
        if arrivals and arrivals[0][0] <= now:
            _, _, name = heapq.heappop(arrivals)
            order.append(("wait", name))
            if name[0] == "P0":
                have.add(("P", 0, name[1]))
            elif name[0] == "halo":
                have.add(name)
            else:
                have.add(every[name][3])
            continue
        ready = [n for n, w in work.items() if n not in done and all(d in have for d in w[1])]
        if ready:
            name = ready[0]
            now += work[name][0]
            done.add(name)
            have.update(work[name][2])
            order.append(("work", name))
            continue
        later = [arrivals[0][0]] if arrivals else []
        waiting = [n for n, m in every.items() if n not in sent and all(d in have for d in m[2])]
        later += [free[every[n][0]] - BACKLOG + 0.01 for n in waiting]
        now = max(now + 0.01, min(later))
    return order, now


def core_kernel(order, h_ref, p_ref, pot_ref, basis_ref, out_ref, a_buf, b_buf, f_buf, o_buf,
                f_acc, s_acc, d_mate, d_chip, d_all, d_got, d_fin,
                basis_buf, halo, eff, part,
                send_sem, recv_sem, local_sem, pin_sem, pin_send, ret_sem, ret_send,
                halo_sem, halo_send, basis_sem):
    row, col = lax.axis_index("row"), lax.axis_index("col")
    x, zl = row // 4, row % 4
    y, zh, c = col // 4, (col // 2) % 2, col % 2
    z = zh * 4 + zl
    basis_copy = pltpu.make_async_copy(basis_ref, basis_buf, basis_sem)
    basis_copy.start()

    def dev(dx=0, dy=0, dz=0, core=None):
        zz = (z + dz) % 8
        core = c if core is None else core
        return (((x + dx) % 4) * 4 + zz % 4, ((y + dy) % 4) * 4 + (zz // 4) * 2 + core)

    def dev_line(q, core):
        return (x * 4 + q, y * 4 + zh * 2 + core)

    barrier = pltpu.get_barrier_semaphore()
    friends = [dev(core=1 - c), dev(dx=1), dev(dx=-1)]
    friends += [dev(dy=j) for j in (1, 2, 3)] + [dev(dz=j) for j in range(1, 8)]
    friends += [dev(dy=j, dz=4) for j in (1, 2, 3)]
    friends += [dev_line((zl + j) % 4, 1 - c) for j in (1, 2, 3)]
    beside = [((row + 1) % 16, col), ((row + 15) % 16, col), (row, (col + 1) % 16),
              (row, (col + 15) % 16)]
    friends += beside
    for friend in friends:
        pl.semaphore_signal(barrier, inc=1, device_id=friend, device_id_type=MESH)
    pl.semaphore_wait(barrier, len(friends))

    names = list(messages())
    index = {n: i for i, n in enumerate(names)}

    def block(s, dy, dz, color):
        zz = (z + dz) % 8
        rows = pl.ds(0, Y_FIRST[s]) if color == "a" else pl.ds(Y_FIRST[s], ROWS - Y_FIRST[s])
        return a_buf.at[s, (y + dy) % 4, zz // 4, zz % 4, rows]

    def block4(s, dz):
        zz = (z + dz) % 8
        return a_buf.at[s, :, zz // 4, zz % 4, pl.ds(0, Y_FIRST[s])]

    def lanes(core):
        return pl.ds(pl.multiple_of(core * WIDE, 128), WIDE)

    def b_slot(dx, rb, core):
        return b_buf.at[(x + dx) % 4, rb, :, core]

    def f_slot(dx, s, core, rbs):
        return f_buf.at[(x + dx) % 4, rbs, s, core]

    FULL, LOW, HIGH = pl.ds(0, 4), pl.ds(0, 2), pl.ds(2, 2)
    PAIR = (LOW, HIGH)

    def ends(name):
        kind = name[0]
        if kind == "Hm":
            s = name[1]
            return (h_ref.at[s, 1 - c], a_buf.at[s, y, zh, zl, :, lanes(c)],
                    a_buf.at[s, y, zh, zl, :, lanes(1 - c)], dev(core=1 - c))
        if kind == "bz+":
            _, s, t = name
            src = block(s, 0, 1 - t, "b")
            return src, src, block(s, 0, -t, "b"), dev(dz=1)
        if kind == "bz-":
            _, s, t = name
            src = block(s, 0, t - 1, "b")
            return src, src, block(s, 0, t, "b"), dev(dz=-1)
        if kind == "by+":
            _, s, dz = name
            src = block(s, 0, dz, "b")
            return src, src, block(s, -1, dz, "b"), dev(dy=1)
        if kind == "by-":
            _, s, dz = name
            src = block(s, 0, dz, "b")
            return src, src, block(s, 1, dz, "b"), dev(dy=-1)
        if kind == "by2":
            _, s, dz = name
            way = 1 if antipode_plus(dz) else -1
            src = block(s, -way, dz, "b")
            return src, src, block(s, 2, dz, "b"), dev(dy=way)
        if kind == "ay+":
            src = block(name[1], 0, 0, "a")
            return src, src, block(name[1], -1, 0, "a"), dev(dy=1)
        if kind == "ay-":
            src = block(name[1], 0, 0, "a")
            return src, src, block(name[1], 1, 0, "a"), dev(dy=-1)
        if kind == "ay2":
            way = 1 if name[1] % 2 == 0 else -1
            src = block(name[1], -way, 0, "a")
            return src, src, block(name[1], 2, 0, "a"), dev(dy=way)
        if kind == "az+":
            _, s, t = name
            src = block4(s, 1 - t)
            return src, src, block4(s, -t), dev(dz=1)
        if kind == "az-":
            _, s, t = name
            src = block4(s, t - 1)
            return src, src, block4(s, t), dev(dz=-1)
        if kind == "Px+":
            src = b_slot(0, name[1], c)
            return src, src, b_slot(-1, name[1], c), dev(dx=1)
        if kind == "Px-":
            src = b_slot(0, name[1], c)
            return src, src, b_slot(1, name[1], c), dev(dx=-1)
        if kind == "Px2":
            way = 1 if name[1] < 2 else -1
            src = b_slot(-way, name[1], c)
            return src, src, b_slot(2, name[1], c), dev(dx=way)
        if kind == "Pm":
            _, dx, rb = name
            src = b_slot(dx, rb, c)
            return src, src, b_slot(dx, rb, 1 - c), dev(core=1 - c)
        if kind == "Fx+":
            _, s, e = name
            src = f_slot(0, s, c, PAIR[e])
            return src, src, f_slot(-1, s, c, PAIR[e]), dev(dx=1)
        if kind == "Fx-":
            _, s, e = name
            src = f_slot(0, s, c, PAIR[e])
            return src, src, f_slot(1, s, c, PAIR[e]), dev(dx=-1)
        if kind == "F2+":
            src = f_slot(-1, name[1], c, LOW)
            return src, src, f_slot(2, name[1], c, LOW), dev(dx=1)
        if kind == "F2-":
            src = f_slot(1, name[1], c, HIGH)
            return src, src, f_slot(2, name[1], c, HIGH), dev(dx=-1)
        if kind == "Fm":
            dx, s = name[1:3]
            rbs = PAIR[name[3]] if len(name) > 3 else FULL
            src = f_slot(dx, s, c, rbs)
            return src, src, f_slot(dx, s, 1 - c, rbs), dev(core=1 - c)
        if kind == "Dm":
            return part.at[:, 1 - c], d_mate, d_mate, dev(core=1 - c)
        if kind == "Dr":
            j = name[1]
            dy, dz = j // 2, 4 * (j % 2)
            to = ((y + dy) % 4) * 2 + (zh + j % 2) % 2
            return d_chip.at[to], d_got.at[j - 1], d_got.at[j - 1], dev(dy=dy, dz=dz)
        if kind == "Dy":
            j = name[1]
            return d_fin, d_all.at[zl, y, zh], d_all.at[zl, (y - j) % 4, zh], dev(dy=j)
        if kind == "Dz":
            j = name[1]
            zz = (z - j) % 8
            src = d_all.at[zl, :, zh]
            return src, src, d_all.at[zz % 4, :, zz // 4], dev(dz=j)
        raise KeyError(name)

    def outgoing(name):
        src, dst, _, target = ends(name)
        i = index[name]
        return pltpu.make_async_remote_copy(
            src_ref=src, dst_ref=dst, send_sem=send_sem.at[i], recv_sem=recv_sem.at[i],
            device_id=target, device_id_type=MESH)

    def incoming(name):
        src, _, land, target = ends(name)
        i = index[name]
        return pltpu.make_async_remote_copy(
            src_ref=land, dst_ref=land, send_sem=send_sem.at[i], recv_sem=recv_sem.at[i],
            device_id=target, device_id_type=MESH)

    to_side = [row < 15, row > 0, col < 15, col > 0]
    from_side = [row > 0, row < 15, col > 0, col < 15]

    def halo_copy(i):
        return pltpu.make_async_remote_copy(
            src_ref=pot_ref, dst_ref=halo.at[i], send_sem=halo_send.at[i],
            recv_sem=halo_sem.at[i], device_id=beside[i], device_id_type=MESH)

    for i in range(4):
        @pl.when(to_side[i])
        def _():
            halo_copy(i).start()

    def wait_halo():
        for i in range(4):
            @pl.when(from_side[i])
            def _():
                halo_copy(i).wait_recv()

            @pl.when(jnp.logical_not(from_side[i]))
            def _():
                halo[i] = jnp.zeros((2, 4, 512), jnp.float32)

    own = [pltpu.make_async_copy(h_ref.at[s, c], a_buf.at[s, y, zh, zl, :, lanes(c)],
                                 local_sem.at[s]) for s in range(STEPS)]
    for copy in own:
        copy.start()

    def p_copy(hf, r):
        q = 2 * c + hf
        src = p_ref.at[hf, :, r]
        here = (q == zl) & (r == c)
        dst = b_buf.at[x, zl, :, r]

        def local():
            return pltpu.make_async_copy(src, dst, pin_sem.at[zl])

        def remote():
            return pltpu.make_async_remote_copy(
                src_ref=src, dst_ref=dst, send_sem=pin_send.at[hf, r], recv_sem=pin_sem.at[zl],
                device_id=dev_line(q, r), device_id_type=MESH)

        return here, local, remote

    def start_p():
        for hf in range(2):
            for r in range(2):
                here, local, remote = p_copy(hf, r)

                @pl.when(here)
                def _():
                    local().start()

                @pl.when(jnp.logical_not(here))
                def _():
                    remote().start()

    def chunk_a(s, yy, zz):
        return a_buf[s, yy, zz].reshape(4 * ROWS, 2 * WIDE)

    def first_product(s, far):
        if not far:
            f_acc[s] = jnp.zeros((4 * ROWS, WIDE), jnp.float32)

        def body(k, carry):
            yy, zz = (y + (k // 2) + 3) % 4, k % 2
            right = b_buf[yy, pl.ds(zz * 2, 2)].reshape(2 * WIDE, WIDE)
            f_acc[s] += jnp.dot(chunk_a(s, yy, zz), right, preferred_element_type=jnp.float32)
            return carry

        lax.fori_loop(6 if far else 0, 8 if far else 6, body, 0)

    def diagonal(rb, s):
        return d_all[rb].reshape(STEPS, ROWS, BLK)[s].astype(jnp.bfloat16)

    def first_finish(s):
        for rb in range(4):
            rows = pl.ds(rb * ROWS, ROWS)
            right = b_buf[x, rb, s].reshape(BLK, WIDE)
            total = f_acc[s, rows] + jnp.dot(diagonal(rb, s), right,
                                             preferred_element_type=jnp.float32)
            f_acc[s, rows] = total
            f_buf[x, rb, s, c] = total.astype(jnp.bfloat16)

    def second_product(s, dx):
        xx = (x + dx) % 4
        tile = slice(s * BLK, (s + 1) * BLK), slice(WIDE + s * BLK, WIDE + (s + 1) * BLK)

        def body(k, carry):
            t, zz = k // 2, k % 2
            left = jnp.concatenate(
                [a_buf[t, xx, zz, :, :, cut].reshape(4 * ROWS, BLK) for cut in tile], axis=1)
            right = jnp.concatenate(
                [f_buf[xx, zz * 2 + e, s].reshape(BLK, WIDE) for e in range(2)], axis=0)
            s_acc[t] += jnp.dot(left, right, preferred_element_type=jnp.float32)
            return carry

        lax.fori_loop(0, 6, body, 0)
        if dx == 0:
            for rb in range(4):
                rows = pl.ds(rb * ROWS, ROWS)
                right = f_buf[x, rb, s].reshape(BLK, WIDE)
                s_acc[s, rows] += jnp.dot(diagonal(rb, s), right,
                                          preferred_element_type=jnp.float32)

    def screen():
        wait_halo()
        zero = jnp.zeros((1, 1), jnp.float32)
        for i in range(2):
            for j in range(4):
                here = pot_ref[i, j:j + 1]
                below = pot_ref[0, j:j + 1] if i else halo[0, 1, j:j + 1]
                above = halo[1, 0, j:j + 1] if i else pot_ref[1, j:j + 1]
                left = pot_ref[i, j - 1:j] if j else halo[2, i, 3:4]
                right = pot_ref[i, j + 1:j + 2] if j < 3 else halo[3, i, 0:1]
                later = jnp.concatenate([here[:, 1:], zero], axis=1)
                earlier = jnp.concatenate([zero, here[:, :-1]], axis=1)
                total = above + below
                total = total + right + left
                total = total + later + earlier
                eff[i, j:j + 1] = here + KAPPA * (total - 6.0 * here)

    def integrate(i):
        if i == 0:
            basis_copy.wait()
            part[...] = jnp.zeros_like(part)

        def body(j, carry):
            cell = 2 * i + j
            table = basis_buf[cell // 4, cell % 4]
            scale = eff[cell // 4, pl.ds(cell % 4, 1)]
            weighted = (table.astype(jnp.float32) * scale).astype(jnp.bfloat16)
            for k in range(3):
                rows = slice(k * BLK, (k + 1) * BLK)
                more = lax.dot_general(weighted[rows], table[rows], (((1,), (1,)), ((), ())),
                                       preferred_element_type=jnp.float32)
                part[k] += more.reshape(2, ROWS, BLK)
            return carry

        lax.fori_loop(0, 2, body, 0)

    def finish_integrals():
        mine = y * 2 + zh
        total = d_chip[mine]
        for j in range(7):
            total = total + d_got[j]
        factor = float(BLK * 2 * 64 * 512) ** -0.5
        d_fin[...] = total * factor
        d_all[zl, y, zh] = total * factor

    def run(name):
        kind = name[0]
        if kind == "Hready":
            own[name[1]].wait()
        elif kind == "E":
            screen()
        elif kind == "I":
            integrate(name[1])
        elif kind == "C1":
            first_product(name[1], name[2])
        elif kind == "Ff":
            first_finish(name[1])
        elif kind == "S":
            second_product(name[1], name[2])
        elif kind == "Dc":
            d_chip[...] = (part[:, c] + d_mate[...]).reshape(8, 24, BLK)
        elif kind == "Df":
            finish_integrals()

    start_p()
    s_acc[...] = jnp.zeros_like(s_acc)
    for what, name in order:
        if what == "send":
            outgoing(name).start()
        elif what == "wait":
            if name[0] == "halo":
                continue
            if name[0] == "P0":
                rb = name[1]
                land = b_buf.at[x, rb, :, c]
                pltpu.make_async_copy(land, land, pin_sem.at[rb]).wait()
            else:
                incoming(name).wait_recv()
        else:
            run(name)

    lane = lax.broadcasted_iota(jnp.int32, (ROWS, BLK), 1)
    quarter = 0.5 * TIME_STEP * TIME_STEP

    def back(rb):
        here = (rb == zl) & (zl // 2 == c)
        src = o_buf.at[rb]
        dst = out_ref.at[zl % 2, :, c]

        def local():
            return pltpu.make_async_copy(src, dst, ret_sem.at[zl % 2, c])

        def remote():
            return pltpu.make_async_remote_copy(
                src_ref=src, dst_ref=dst, send_sem=ret_send.at[rb],
                recv_sem=ret_sem.at[zl % 2, c],
                device_id=dev_line(rb, zl // 2), device_id_type=MESH)

        return here, local, remote

    for rb in range(4):
        rows = pl.ds(rb * ROWS, ROWS)
        for s in range(STEPS):
            base = b_buf[x, rb, s, c].astype(jnp.float32)
            f = f_acc[s, rows]
            mixed = f[:, 2 * BLK:]
            turned = pltpu.roll(mixed, BLK // 2, 1)
            turn = jnp.concatenate(
                [f[:, BLK:2 * BLK], -f[:, :BLK], jnp.where(lane < BLK // 2, turned, -turned)],
                axis=1)
            o_buf[rb, s] = (base + TIME_STEP * turn - quarter * s_acc[s, rows]).astype(jnp.bfloat16)
        here, local, remote = back(rb)

        @pl.when(here)
        def _():
            local().start()

        @pl.when(jnp.logical_not(here))
        def _():
            remote().start()

    for hf in range(2):
        for r in range(2):
            land = out_ref.at[hf, :, r]
            pltpu.make_async_copy(land, land, ret_sem.at[hf, r]).wait()

    for what, name in order:
        if what == "send":
            outgoing(name).wait_send()
    for hf in range(2):
        for r in range(2):
            here, _, remote = p_copy(hf, r)

            @pl.when(jnp.logical_not(here))
            def _():
                remote().wait_send()
    for rb in range(4):
        here, _, remote = back(rb)

        @pl.when(jnp.logical_not(here))
        def _():
            remote().wait_send()
    for i in range(4):
        @pl.when(to_side[i])
        def _():
            halo_copy(i).wait_send()


def propagate(h, p, potential, basis):
    order, _ = schedule()
    total = len(messages())
    bf, f32 = jnp.bfloat16, jnp.float32
    any_space = pl.BlockSpec(memory_space=pl.ANY)
    vmem = pl.BlockSpec(memory_space=pltpu.VMEM)
    return pl.pallas_call(
        functools.partial(core_kernel, order),
        out_shape=jax.ShapeDtypeStruct((2, STEPS, 2, ROWS, WIDE), bf),
        in_specs=[any_space, any_space, vmem, any_space],
        out_specs=any_space,
        scratch_shapes=[
            pltpu.VMEM((STEPS, 4, 2, 4, ROWS, 2 * WIDE), bf),
            pltpu.VMEM((4, 4, STEPS, 2, ROWS, WIDE), bf),
            pltpu.VMEM((4, 4, STEPS, 2, ROWS, WIDE), bf),
            pltpu.VMEM((4, STEPS, ROWS, WIDE), bf),
            pltpu.VMEM((STEPS, 4 * ROWS, WIDE), f32),
            pltpu.VMEM((STEPS, 4 * ROWS, WIDE), f32),
            pltpu.VMEM((STEPS, ROWS, BLK), f32),
            pltpu.VMEM((8, 24, BLK), f32),
            pltpu.VMEM((4, 4, 2, 24, BLK), f32),
            pltpu.VMEM((7, 24, BLK), f32),
            pltpu.VMEM((24, BLK), f32),
            pltpu.VMEM((2, 4, WIDE, 512), bf),
            pltpu.VMEM((4, 2, 4, 512), f32),
            pltpu.VMEM((2, 4, 512), f32),
            pltpu.VMEM((STEPS, 2, ROWS, BLK), f32),
            pltpu.SemaphoreType.DMA((total,)),
            pltpu.SemaphoreType.DMA((total,)),
            pltpu.SemaphoreType.DMA((STEPS,)),
            pltpu.SemaphoreType.DMA((4,)),
            pltpu.SemaphoreType.DMA((2, 2)),
            pltpu.SemaphoreType.DMA((2, 2)),
            pltpu.SemaphoreType.DMA((4,)),
            pltpu.SemaphoreType.DMA((4,)),
            pltpu.SemaphoreType.DMA((4,)),
            pltpu.SemaphoreType.DMA,
        ],
        compiler_params=pltpu.CompilerParams(
            collective_id=0, has_side_effects=True, vmem_limit_bytes=48 << 20),
        name="propagate",
    )(h, p, potential, basis)


def shards(potential, basis, hamiltonian, density, hmask, pmask):
    row_start = lax.axis_index("row") * 3
    col_start = lax.axis_index("col") * 3
    hpattern = lax.dynamic_slice(hmask, (row_start, col_start), (3, 3))
    ppattern = lax.dynamic_slice(pmask, (row_start, col_start), (3, 3))
    masked_h = (
        hamiltonian.reshape(3, BLK, 3, BLK) * hpattern[:, None, :, None].astype(jnp.bfloat16)
    ).reshape(STEPS, 2, ROWS, WIDE)
    masked_p = (
        density.reshape(2, 3, BLK, 3, BLK) * ppattern[None, :, None, :, None].astype(jnp.bfloat16)
    ).reshape(2, WIDE, WIDE)
    units = jnp.stack([
        jnp.concatenate(
            [masked_p[0, :, t * BLK:(t + 1) * BLK], masked_p[1, :, t * BLK:(t + 1) * BLK],
             masked_p[0, :, 256 + 64 * t:320 + 64 * t], masked_p[1, :, 256 + 64 * t:320 + 64 * t]],
            axis=1)
        for t in range(2)
    ]).reshape(2, STEPS, 2, ROWS, WIDE)
    result = propagate(masked_h, units, potential, basis).reshape(2, WIDE, WIDE)
    whole = jnp.stack([
        jnp.concatenate(
            [result[0, :, t * BLK:(t + 1) * BLK], result[1, :, t * BLK:(t + 1) * BLK],
             result[0, :, 256 + 64 * t:320 + 64 * t], result[1, :, 256 + 64 * t:320 + 64 * t]],
            axis=1)
        for t in range(2)
    ])
    whole = whole.reshape(2, 3, BLK, 3, BLK) * ppattern[None, :, None, :, None].astype(jnp.bfloat16)
    return whole.reshape(2, WIDE, WIDE)


def solution(mesh):
    in_specs = (
        P("row", "col", None),
        P("row", "col", None, None),
        P("row", "col"),
        P(None, "row", "col"),
        P(),
        P(),
    )
    out_specs = P(None, "row", "col")
    return jax.shard_map(shards, mesh=mesh, in_specs=in_specs, out_specs=out_specs, check_vma=False)
```

```python
import functools
import heapq

import jax
import jax.numpy as jnp
from jax import lax
from jax.experimental import pallas as pl
from jax.experimental.pallas import tpu as pltpu
from jax.sharding import PartitionSpec as P

BLK = 128
KAPPA = 0.4
TIME_STEP = 0.5
MESH = pl.DeviceIdType.MESH

STEPS = 3
ROWS = 64
CHUNKS = ((0, 0, 64, 16), (1, 0, 64, 32), (2, 0, 32, 16), (2, 32, 32, 0))
WIDE = 384


def plus_hops(s):
    return 4 if s % 2 == 0 else 3


def antipode_plus(dz):
    return dz % 2 == 0


def messages():
    out = {}
    for s in range(STEPS):
        out["Hm", s] = ("m", 48, [], ("H", s))
    for s, (_, _, rows, y_first) in enumerate(CHUNKS):
        a_kb, b_kb = y_first * 1.5, (rows - y_first) * 1.5
        up, down = plus_hops(s), 7 - plus_hops(s)
        for t in range(1, up + 1):
            out["bz+", s, t] = ("z+", b_kb, [("b", s, 0, 1 - t)], ("b", s, 0, -t))
        for t in range(1, down + 1):
            out["bz-", s, t] = ("z-", b_kb, [("b", s, 0, t - 1)], ("b", s, 0, t))
        for dz in range(-up, down + 1):
            out["by+", s, dz] = ("y+", b_kb, [("b", s, 0, dz)], ("b", s, -1, dz))
            out["by-", s, dz] = ("y-", b_kb, [("b", s, 0, dz)], ("b", s, 1, dz))
            if antipode_plus(dz):
                out["by2", s, dz] = ("y+", b_kb, [("b", s, -1, dz)], ("b", s, 2, dz))
            else:
                out["by2", s, dz] = ("y-", b_kb, [("b", s, 1, dz)], ("b", s, 2, dz))
        if not y_first:
            continue
        out["ay+", s] = ("y+", a_kb, [("a", s, 0)], ("a", s, -1))
        out["ay-", s] = ("y-", a_kb, [("a", s, 0)], ("a", s, 1))
        if s % 2 == 0:
            out["ay2", s] = ("y+", a_kb, [("a", s, -1)], ("a", s, 2))
        else:
            out["ay2", s] = ("y-", a_kb, [("a", s, 1)], ("a", s, 2))
        whole = [("a", s, 0), ("a", s, -1), ("a", s, 1), ("a", s, 2)]
        for t in range(1, up + 1):
            needs = whole if t == 1 else [("A4", s, 1 - t)]
            out["az+", s, t] = ("z+", 4 * a_kb, needs, ("A4", s, -t))
        for t in range(1, down + 1):
            needs = whole if t == 1 else [("A4", s, t - 1)]
            out["az-", s, t] = ("z-", 4 * a_kb, needs, ("A4", s, t))
    for rb in range(4):
        out["Px+", rb] = ("x+", 144, [("P", 0, rb)], ("P", -1, rb))
        out["Px-", rb] = ("x-", 144, [("P", 0, rb)], ("P", 1, rb))
        if rb < 2:
            out["Px2", rb] = ("x+", 144, [("P", -1, rb)], ("P", 2, rb))
        else:
            out["Px2", rb] = ("x-", 144, [("P", 1, rb)], ("P", 2, rb))
        for dx in (0, -1, 1, 2):
            out["Pm", dx, rb] = ("m", 144, [("P", dx, rb)], ("Pm", dx, rb))
    for s, (_, _, rows, _) in enumerate(CHUNKS):
        kb = rows * 1.5
        for e in (0, 1):
            out["Fx+", s, e] = ("x+", kb, [("F", 0, s)], ("F", -1, s, e))
            out["Fx-", s, 1 - e] = ("x-", kb, [("F", 0, s)], ("F", 1, s, 1 - e))
        out["F2+", s] = ("x+", kb, [("F", -1, s, 0)], ("F", 2, s, 0))
        out["F2-", s] = ("x-", kb, [("F", 1, s, 1)], ("F", 2, s, 1))
        out["Fm", 0, s] = ("m", 2 * kb, [("F", 0, s)], ("Fm", 0, s))
        for dx in (-1, 1, 2):
            for e in (0, 1):
                out["Fm", dx, s, e] = ("m", kb, [("F", dx, s, e)], ("Fm", dx, s, e))
    out["Dm",] = ("m", 96, [("I", i) for i in range(4)], ("Dm",))
    for j in range(1, 4):
        out["Dr", j] = ("y-" if j == 3 else "y+", 12 if j != 2 else 24, [("Dc",)], ("Dr", j))
    for k in (1, -1, 2, -2, 3, -3, 4):
        out["Dz", k] = ("z+" if k > 0 else "z-", 12 * abs(k), [("Dl",)], ("Dz", k))
    for j in range(1, 4):
        out["Dy", j] = ("y-" if j == 3 else "y+", 48 if j != 2 else 96, [("Df",)], ("Dy", j))
    return out


def tasks():
    out = {}
    for s in range(STEPS):
        gives = [(k, i, 0, 0) if k == "b" else (k, i, 0)
                 for i, chunk in enumerate(CHUNKS) if chunk[0] == s for k in "ba"]
        out["Hready", s] = (0.05, [("H", s)], gives)
    every_p = [("P", dx, rb) for dx in (0, -1, 1, 2) for rb in range(4)]
    every_p += [("Pm", dx, rb) for dx in (0, -1, 1, 2) for rb in range(4)]
    every_d = [("Dy", i) for i in (1, 2, 3)] + [("Df",)]
    for s, (_, _, rows, y_first) in enumerate(CHUNKS):
        up, down = plus_hops(s), 7 - plus_hops(s)
        near = [("b", s, dy, dz) for dy in (0, -1, 1) for dz in range(-up, down + 1)]
        if y_first:
            near += [("A4", s, dz) for dz in range(-up, down + 1) if dz] + [("a", s, 2)]
        far = [("b", s, 2, dz) for dz in range(-up, down + 1)]
        out["C1", s, 0] = (0.2 + 0.035 * rows, near + every_p, [("C1", s, 0)])
        out["C1", s, 1] = (0.1 + 0.011 * rows, far + [("C1", s, 0)], [("C1", s, 1)])
        out["Ff", s] = (0.5, [("C1", s, 1)] + every_d, [("F", 0, s)])
    out["E",] = (0.5, [("halo",)], [("E",)])
    for i in range(4):
        out["I", i] = (1.5, [("E",)], [("I", i)])
    out["Dc",] = (0.2, [("Dm",)], [("Dc",)])
    out["Dl",] = (0.2, [("Dc",)] + [("Dr", j) for j in (1, 2, 3)], [("Dl",)])
    out["Df",] = (0.2, [("Dl",)] + [("Dz", k) for k in (1, -1, 2, -2, 3, -3, 4)], [("Df",)])
    all_a = [("C1", s, 1) for s in range(len(CHUNKS))]
    for t in range(STEPS):
        mine = [s for s, chunk in enumerate(CHUNKS) if chunk[0] == t]
        needs = {0: [(k, 0, s) for k in ("F", "Fm") for s in mine]}
        for dx in (-1, 1, 2):
            needs[dx] = [(k, dx, s, e) for k in ("F", "Fm") for e in (0, 1) for s in mine]
        if t < STEPS - 1:
            early = [("C1", 0, 1), ("C1", 1, 1)] + sum(needs.values(), [])
            out["S", t, 9, 0, 2] = (2.2, early, [("S", t, 0)])
            out["S", t, 9, 2, 3] = (1.1, early + all_a, [("S", t, 1)])
            continue
        for dx in (0, -1, 1, 2):
            out["S", t, dx, 0, 3] = (0.8, all_a + needs[dx], [("S", t, dx)])
    return out


RATE = {"m": 200.0}
LINK_RATE = 42.0
BACKLOG = 4.0
D_WAIT = {"Dr": 5.0, "Dz": 6.0, "Dy": 5.0}


def rank_of(name):
    kind = name[0]
    if kind in ("Hm", "Dm", "Dr", "Dy", "Dz"):
        return (-1, 0)
    if kind[0] in "PF":
        return (0, 0)
    return (name[1], 0 if kind in ("bz+", "bz-", "ay+", "ay-", "ay2") else 1)


def schedule():
    every, work = messages(), tasks()
    given_by = {m[3]: n for n, m in every.items()}
    have, sent, done = set(), set(), set()
    free = {}
    arrivals = []
    order = []
    now = 0.0
    free["z+"] = free["z-"] = 2 * 144 / LINK_RATE
    for rb in range(4):
        heapq.heappush(arrivals, (20.0 + rb, 0, ("P0", rb)))
    heapq.heappush(arrivals, (4.0, 0, ("halo",)))
    count = 0

    def issue():
        nonlocal count
        ready = [n for n, m in every.items() if n not in sent and all(d in have for d in m[2])]
        ready.sort(key=rank_of)
        for name in ready:
            link, size, _, _ = every[name]
            start = max(now, free.get(link, 0.0))
            if start - now > BACKLOG and link != "m" and name[0][0] != "D":
                continue
            end = start + size / RATE.get(link, LINK_RATE)
            free[link] = end
            sent.add(name)
            count += 1
            wait = D_WAIT.get(name[0], 1.0 if link == "m" else 1.8)
            heapq.heappush(arrivals, (end + wait, count, name))
            order.append(("send", name))

    while len(done) < len(work) or arrivals:
        issue()
        if arrivals and arrivals[0][0] <= now:
            _, _, name = heapq.heappop(arrivals)
            order.append(("wait", name))
            if name[0] == "P0":
                have.add(("P", 0, name[1]))
            elif name[0] == "halo":
                have.add(name)
            else:
                have.add(every[name][3])
            continue
        ready = [n for n, w in work.items() if n not in done and all(d in have for d in w[1])]
        if ready:
            name = ready[0]
            now += work[name][0]
            done.add(name)
            have.update(work[name][2])
            order.append(("work", name))
            continue
        later = [arrivals[0][0]] if arrivals else []
        waiting = [n for n, m in every.items() if n not in sent and all(d in have for d in m[2])]
        later += [free[every[n][0]] - BACKLOG + 0.01 for n in waiting]
        now = max(now + 0.01, min(later))
    return order, now


def core_kernel(order, h_ref, p_ref, pot_ref, basis_ref, out_ref, a_buf, b_buf, f_buf, o_buf,
                f_acc, s_acc, d_mate, d_chip, d_all, d_got, d_line,
                basis_buf, halo, eff, part,
                send_sem, recv_sem, local_sem, pin_sem, pin_send, ret_sem, ret_send,
                halo_sem, halo_send, basis_sem):
    row, col = lax.axis_index("row"), lax.axis_index("col")
    x, zl = row // 4, row % 4
    y, zh, c = col // 4, (col // 2) % 2, col % 2
    z = zh * 4 + zl
    basis_copy = pltpu.make_async_copy(basis_ref, basis_buf, basis_sem)
    basis_copy.start()

    def dev(dx=0, dy=0, dz=0, core=None):
        zz = (z + dz) % 8
        core = c if core is None else core
        return (((x + dx) % 4) * 4 + zz % 4, ((y + dy) % 4) * 4 + (zz // 4) * 2 + core)

    def dev_line(q, core):
        return (x * 4 + q, y * 4 + zh * 2 + core)

    barrier = pltpu.get_barrier_semaphore()
    friends = [dev(core=1 - c), dev(dx=1), dev(dx=-1)]
    friends += [dev(dy=j) for j in (1, 2, 3)] + [dev(dz=j) for j in range(1, 8)]
    friends += [dev(dy=j, dz=4) for j in (1, 2, 3)]
    friends += [dev_line((zl + j) % 4, 1 - c) for j in (1, 2, 3)]
    beside = [((row + 1) % 16, col), ((row + 15) % 16, col), (row, (col + 1) % 16),
              (row, (col + 15) % 16)]
    friends += beside
    for friend in friends:
        pl.semaphore_signal(barrier, inc=1, device_id=friend, device_id_type=MESH)
    pl.semaphore_wait(barrier, len(friends))

    names = list(messages())
    index = {n: i for i, n in enumerate(names)}

    def block(s, dy, dz, color):
        zz = (z + dz) % 8
        tile, first, count, y_first = CHUNKS[s]
        rows = pl.ds(first, y_first) if color == "a" else pl.ds(first + y_first, count - y_first)
        return a_buf.at[tile, (y + dy) % 4, zz // 4, zz % 4, rows]

    def block4(s, dz):
        zz = (z + dz) % 8
        tile, first, _, y_first = CHUNKS[s]
        return a_buf.at[tile, :, zz // 4, zz % 4, pl.ds(first, y_first)]

    def lanes(core):
        return pl.ds(pl.multiple_of(core * WIDE, 128), WIDE)

    def b_slot(dx, rb, core):
        return b_buf.at[(x + dx) % 4, rb, :, core]

    def f_slot(dx, s, core, rbs):
        tile, first, count, _ = CHUNKS[s]
        return f_buf.at[(x + dx) % 4, rbs, tile, core, pl.ds(first, count)]

    FULL, LOW, HIGH = pl.ds(0, 4), pl.ds(0, 2), pl.ds(2, 2)
    PAIR = (LOW, HIGH)

    def ends(name):
        kind = name[0]
        if kind == "Hm":
            s = name[1]
            return (h_ref.at[s, 1 - c], a_buf.at[s, y, zh, zl, :, lanes(c)],
                    a_buf.at[s, y, zh, zl, :, lanes(1 - c)], dev(core=1 - c))
        if kind == "bz+":
            _, s, t = name
            src = block(s, 0, 1 - t, "b")
            return src, src, block(s, 0, -t, "b"), dev(dz=1)
        if kind == "bz-":
            _, s, t = name
            src = block(s, 0, t - 1, "b")
            return src, src, block(s, 0, t, "b"), dev(dz=-1)
        if kind == "by+":
            _, s, dz = name
            src = block(s, 0, dz, "b")
            return src, src, block(s, -1, dz, "b"), dev(dy=1)
        if kind == "by-":
            _, s, dz = name
            src = block(s, 0, dz, "b")
            return src, src, block(s, 1, dz, "b"), dev(dy=-1)
        if kind == "by2":
            _, s, dz = name
            way = 1 if antipode_plus(dz) else -1
            src = block(s, -way, dz, "b")
            return src, src, block(s, 2, dz, "b"), dev(dy=way)
        if kind == "ay+":
            src = block(name[1], 0, 0, "a")
            return src, src, block(name[1], -1, 0, "a"), dev(dy=1)
        if kind == "ay-":
            src = block(name[1], 0, 0, "a")
            return src, src, block(name[1], 1, 0, "a"), dev(dy=-1)
        if kind == "ay2":
            way = 1 if name[1] % 2 == 0 else -1
            src = block(name[1], -way, 0, "a")
            return src, src, block(name[1], 2, 0, "a"), dev(dy=way)
        if kind == "az+":
            _, s, t = name
            src = block4(s, 1 - t)
            return src, src, block4(s, -t), dev(dz=1)
        if kind == "az-":
            _, s, t = name
            src = block4(s, t - 1)
            return src, src, block4(s, t), dev(dz=-1)
        if kind == "Px+":
            src = b_slot(0, name[1], c)
            return src, src, b_slot(-1, name[1], c), dev(dx=1)
        if kind == "Px-":
            src = b_slot(0, name[1], c)
            return src, src, b_slot(1, name[1], c), dev(dx=-1)
        if kind == "Px2":
            way = 1 if name[1] < 2 else -1
            src = b_slot(-way, name[1], c)
            return src, src, b_slot(2, name[1], c), dev(dx=way)
        if kind == "Pm":
            _, dx, rb = name
            src = b_slot(dx, rb, c)
            return src, src, b_slot(dx, rb, 1 - c), dev(core=1 - c)
        if kind == "Fx+":
            _, s, e = name
            src = f_slot(0, s, c, PAIR[e])
            return src, src, f_slot(-1, s, c, PAIR[e]), dev(dx=1)
        if kind == "Fx-":
            _, s, e = name
            src = f_slot(0, s, c, PAIR[e])
            return src, src, f_slot(1, s, c, PAIR[e]), dev(dx=-1)
        if kind == "F2+":
            src = f_slot(-1, name[1], c, LOW)
            return src, src, f_slot(2, name[1], c, LOW), dev(dx=1)
        if kind == "F2-":
            src = f_slot(1, name[1], c, HIGH)
            return src, src, f_slot(2, name[1], c, HIGH), dev(dx=-1)
        if kind == "Fm":
            dx, s = name[1:3]
            rbs = PAIR[name[3]] if len(name) > 3 else FULL
            src = f_slot(dx, s, c, rbs)
            return src, src, f_slot(dx, s, 1 - c, rbs), dev(core=1 - c)
        if kind == "Dm":
            return part.at[:, 1 - c], d_mate, d_mate, dev(core=1 - c)
        if kind == "Dr":
            j = name[1]
            return d_chip.at[(y + j) % 4], d_got.at[j - 1], d_got.at[j - 1], dev(dy=j)
        if kind == "Dz":
            k = name[1]
            zz = (z - k) % 8
            src = d_line.at[zh, zl]
            return src, src, d_line.at[zz // 4, zz % 4], dev(dz=k)
        if kind == "Dy":
            j = name[1]
            src = d_all.at[:, y]
            return src, src, d_all.at[:, (y - j) % 4], dev(dy=j)
        raise KeyError(name)

    def outgoing(name):
        src, dst, _, target = ends(name)
        i = index[name]
        return pltpu.make_async_remote_copy(
            src_ref=src, dst_ref=dst, send_sem=send_sem.at[i], recv_sem=recv_sem.at[i],
            device_id=target, device_id_type=MESH)

    def incoming(name):
        src, _, land, target = ends(name)
        i = index[name]
        return pltpu.make_async_remote_copy(
            src_ref=land, dst_ref=land, send_sem=send_sem.at[i], recv_sem=recv_sem.at[i],
            device_id=target, device_id_type=MESH)

    to_side = [row < 15, row > 0, col < 15, col > 0]
    from_side = [row > 0, row < 15, col > 0, col < 15]

    def halo_copy(i):
        return pltpu.make_async_remote_copy(
            src_ref=pot_ref, dst_ref=halo.at[i], send_sem=halo_send.at[i],
            recv_sem=halo_sem.at[i], device_id=beside[i], device_id_type=MESH)

    for i in range(4):
        @pl.when(to_side[i])
        def _():
            halo_copy(i).start()

    def wait_halo():
        for i in range(4):
            @pl.when(from_side[i])
            def _():
                halo_copy(i).wait_recv()

            @pl.when(jnp.logical_not(from_side[i]))
            def _():
                halo[i] = jnp.zeros((2, 4, 512), jnp.float32)

    own = [pltpu.make_async_copy(h_ref.at[s, c], a_buf.at[s, y, zh, zl, :, lanes(c)],
                                 local_sem.at[s]) for s in range(STEPS)]
    for copy in own:
        copy.start()

    def p_copy(hf, r):
        q = 2 * c + hf
        src = p_ref.at[hf, :, r]
        here = (q == zl) & (r == c)
        dst = b_buf.at[x, zl, :, r]

        def local():
            return pltpu.make_async_copy(src, dst, pin_sem.at[zl])

        def remote():
            return pltpu.make_async_remote_copy(
                src_ref=src, dst_ref=dst, send_sem=pin_send.at[hf, r], recv_sem=pin_sem.at[zl],
                device_id=dev_line(q, r), device_id_type=MESH)

        return here, local, remote

    def start_p():
        for hf in range(2):
            for r in range(2):
                here, local, remote = p_copy(hf, r)

                @pl.when(here)
                def _():
                    local().start()

                @pl.when(jnp.logical_not(here))
                def _():
                    remote().start()

    def first_product(s, far):
        tile, first, count, _ = CHUNKS[s]
        rows = slice(first, first + count)
        if not far:
            f_acc[tile, :, rows] = jnp.zeros((4, count, WIDE), jnp.float32)

        def body(k, carry):
            yy, zz = (y + (k // 2) + 3) % 4, k % 2
            left = a_buf[tile, yy, zz, :, rows].reshape(4 * count, 2 * WIDE)
            right = b_buf[yy, pl.ds(zz * 2, 2)].reshape(2 * WIDE, WIDE)
            more = jnp.dot(left, right, preferred_element_type=jnp.float32)
            f_acc[tile, :, rows] += more.reshape(4, count, WIDE)
            return carry

        lax.fori_loop(6 if far else 0, 8 if far else 6, body, 0)

    def diagonal(rb, s):
        return d_all[rb].astype(jnp.float32).reshape(STEPS, ROWS, BLK)[s].astype(jnp.bfloat16)

    def first_finish(s):
        tile, first, count, _ = CHUNKS[s]
        rows = slice(first, first + count)
        for rb in range(4):
            right = b_buf[x, rb, tile].reshape(BLK, WIDE)
            total = f_acc[tile, rb, rows] + jnp.dot(diagonal(rb, tile)[rows], right,
                                                    preferred_element_type=jnp.float32)
            f_acc[tile, rb, rows] = total
            f_buf[x, rb, tile, c, rows] = total.astype(jnp.bfloat16)

    def second_product(s, dx, low, high):
        cuts = [slice(e * WIDE + s * BLK, e * WIDE + (s + 1) * BLK) for e in range(2)]

        def body(k, carry):
            xx, t = (x + (k // (high - low) if dx == 9 else dx)) % 4, low + k % (high - low)
            left = jnp.concatenate(
                [a_buf[t, xx, zz, :, :, cut].reshape(4 * ROWS, BLK)
                 for zz in range(2) for cut in cuts], axis=1)
            right = f_buf[xx, :, s].reshape(4 * BLK, WIDE)
            more = jnp.dot(left, right, preferred_element_type=jnp.float32)
            s_acc[t] += more.reshape(4, ROWS, WIDE)
            return carry

        lax.fori_loop(0, (4 if dx == 9 else 1) * (high - low), body, 0)
        if dx in (0, 9) and low <= s < high:
            for rb in range(4):
                right = f_buf[x, rb, s].reshape(BLK, WIDE)
                s_acc[s, rb] += jnp.dot(diagonal(rb, s), right,
                                        preferred_element_type=jnp.float32)

    def screen():
        wait_halo()
        zero = jnp.zeros((1, 1), jnp.float32)
        for i in range(2):
            for j in range(4):
                here = pot_ref[i, j:j + 1]
                below = pot_ref[0, j:j + 1] if i else halo[0, 1, j:j + 1]
                above = halo[1, 0, j:j + 1] if i else pot_ref[1, j:j + 1]
                left = pot_ref[i, j - 1:j] if j else halo[2, i, 3:4]
                right = pot_ref[i, j + 1:j + 2] if j < 3 else halo[3, i, 0:1]
                later = jnp.concatenate([here[:, 1:], zero], axis=1)
                earlier = jnp.concatenate([zero, here[:, :-1]], axis=1)
                total = above + below
                total = total + right + left
                total = total + later + earlier
                eff[i, j:j + 1] = here + KAPPA * (total - 6.0 * here)

    def integrate(i):
        if i == 0:
            basis_copy.wait()
            part[...] = jnp.zeros_like(part)

        def body(j, carry):
            cell = 2 * i + j
            table = basis_buf[cell // 4, cell % 4]
            scale = eff[cell // 4, pl.ds(cell % 4, 1)]
            weighted = (table.astype(jnp.float32) * scale).astype(jnp.bfloat16)
            for k in range(3):
                rows = slice(k * BLK, (k + 1) * BLK)
                more = lax.dot_general(weighted[rows], table[rows], (((1,), (1,)), ((), ())),
                                       preferred_element_type=jnp.float32)
                part[k] += more.reshape(2, ROWS, BLK)
            return carry

        lax.fori_loop(0, 2, body, 0)

    def line_integrals():
        total = d_chip[y].astype(jnp.float32)
        for j in range(3):
            total = total + d_got[j].astype(jnp.float32)
        d_line[zh, zl] = total.astype(jnp.bfloat16)

    def finish_integrals():
        factor = float(BLK * 2 * 64 * 512) ** -0.5
        total = d_line[0].astype(jnp.float32) + d_line[1].astype(jnp.float32)
        d_all[:, y] = (total * factor).astype(jnp.bfloat16)

    def run(name):
        kind = name[0]
        if kind == "Hready":
            own[name[1]].wait()
        elif kind == "E":
            screen()
        elif kind == "I":
            integrate(name[1])
        elif kind == "C1":
            first_product(name[1], name[2])
        elif kind == "Ff":
            first_finish(name[1])
        elif kind == "S":
            second_product(*name[1:])
        elif kind == "Dc":
            d_chip[...] = (part[:, c] + d_mate[...]).reshape(4, 48, BLK).astype(jnp.bfloat16)
        elif kind == "Dl":
            line_integrals()
        elif kind == "Df":
            finish_integrals()

    start_p()
    s_acc[...] = jnp.zeros_like(s_acc)
    for what, name in order:
        if what == "send":
            outgoing(name).start()
        elif what == "wait":
            if name[0] == "halo":
                continue
            if name[0] == "P0":
                rb = name[1]
                land = b_buf.at[x, rb, :, c]
                pltpu.make_async_copy(land, land, pin_sem.at[rb]).wait()
            else:
                incoming(name).wait_recv()
        else:
            run(name)

    lane = lax.broadcasted_iota(jnp.int32, (ROWS, BLK), 1)
    quarter = 0.5 * TIME_STEP * TIME_STEP

    def back(rb):
        here = (rb == zl) & (zl // 2 == c)
        src = o_buf.at[rb]
        dst = out_ref.at[zl % 2, :, c]

        def local():
            return pltpu.make_async_copy(src, dst, ret_sem.at[zl % 2, c])

        def remote():
            return pltpu.make_async_remote_copy(
                src_ref=src, dst_ref=dst, send_sem=ret_send.at[rb],
                recv_sem=ret_sem.at[zl % 2, c],
                device_id=dev_line(rb, zl // 2), device_id_type=MESH)

        return here, local, remote

    for rb in range(4):
        for s in range(STEPS):
            base = b_buf[x, rb, s, c].astype(jnp.float32)
            f = f_acc[s, rb]
            mixed = f[:, 2 * BLK:]
            turned = pltpu.roll(mixed, BLK // 2, 1)
            turn = jnp.concatenate(
                [f[:, BLK:2 * BLK], -f[:, :BLK], jnp.where(lane < BLK // 2, turned, -turned)],
                axis=1)
            o_buf[rb, s] = (base + TIME_STEP * turn - quarter * s_acc[s, rb]).astype(jnp.bfloat16)
        here, local, remote = back(rb)

        @pl.when(here)
        def _():
            local().start()

        @pl.when(jnp.logical_not(here))
        def _():
            remote().start()

    for hf in range(2):
        for r in range(2):
            land = out_ref.at[hf, :, r]
            pltpu.make_async_copy(land, land, ret_sem.at[hf, r]).wait()

    for what, name in order:
        if what == "send":
            outgoing(name).wait_send()
    for hf in range(2):
        for r in range(2):
            here, _, remote = p_copy(hf, r)

            @pl.when(jnp.logical_not(here))
            def _():
                remote().wait_send()
    for rb in range(4):
        here, _, remote = back(rb)

        @pl.when(jnp.logical_not(here))
        def _():
            remote().wait_send()
    for i in range(4):
        @pl.when(to_side[i])
        def _():
            halo_copy(i).wait_send()


def propagate(h, p, potential, basis):
    order, _ = schedule()
    total = len(messages())
    bf, f32 = jnp.bfloat16, jnp.float32
    any_space = pl.BlockSpec(memory_space=pl.ANY)
    vmem = pl.BlockSpec(memory_space=pltpu.VMEM)
    return pl.pallas_call(
        functools.partial(core_kernel, order),
        out_shape=jax.ShapeDtypeStruct((2, STEPS, 2, ROWS, WIDE), bf),
        in_specs=[any_space, any_space, vmem, any_space],
        out_specs=any_space,
        scratch_shapes=[
            pltpu.VMEM((STEPS, 4, 2, 4, ROWS, 2 * WIDE), bf),
            pltpu.VMEM((4, 4, STEPS, 2, ROWS, WIDE), bf),
            pltpu.VMEM((4, 4, STEPS, 2, ROWS, WIDE), bf),
            pltpu.VMEM((4, STEPS, ROWS, WIDE), bf),
            pltpu.VMEM((STEPS, 4, ROWS, WIDE), f32),
            pltpu.VMEM((STEPS, 4, ROWS, WIDE), f32),
            pltpu.VMEM((STEPS, ROWS, BLK), f32),
            pltpu.VMEM((4, 48, BLK), bf),
            pltpu.VMEM((4, 4, 48, BLK), bf),
            pltpu.VMEM((3, 48, BLK), bf),
            pltpu.VMEM((2, 4, 48, BLK), bf),
            pltpu.VMEM((2, 4, WIDE, 512), bf),
            pltpu.VMEM((4, 2, 4, 512), f32),
            pltpu.VMEM((2, 4, 512), f32),
            pltpu.VMEM((STEPS, 2, ROWS, BLK), f32),
            pltpu.SemaphoreType.DMA((total,)),
            pltpu.SemaphoreType.DMA((total,)),
            pltpu.SemaphoreType.DMA((STEPS,)),
            pltpu.SemaphoreType.DMA((4,)),
            pltpu.SemaphoreType.DMA((2, 2)),
            pltpu.SemaphoreType.DMA((2, 2)),
            pltpu.SemaphoreType.DMA((4,)),
            pltpu.SemaphoreType.DMA((4,)),
            pltpu.SemaphoreType.DMA((4,)),
            pltpu.SemaphoreType.DMA,
        ],
        compiler_params=pltpu.CompilerParams(
            collective_id=0, has_side_effects=True, vmem_limit_bytes=60 << 20),
        name="propagate",
    )(h, p, potential, basis)


def shards(potential, basis, hamiltonian, density, hmask, pmask):
    row_start = lax.axis_index("row") * 3
    col_start = lax.axis_index("col") * 3
    hpattern = lax.dynamic_slice(hmask, (row_start, col_start), (3, 3))
    ppattern = lax.dynamic_slice(pmask, (row_start, col_start), (3, 3))
    masked_h = (
        hamiltonian.reshape(3, BLK, 3, BLK) * hpattern[:, None, :, None].astype(jnp.bfloat16)
    ).reshape(STEPS, 2, ROWS, WIDE)
    masked_p = (
        density.reshape(2, 3, BLK, 3, BLK) * ppattern[None, :, None, :, None].astype(jnp.bfloat16)
    ).reshape(2, WIDE, WIDE)
    units = jnp.stack([
        jnp.concatenate(
            [masked_p[0, :, t * BLK:(t + 1) * BLK], masked_p[1, :, t * BLK:(t + 1) * BLK],
             masked_p[0, :, 256 + 64 * t:320 + 64 * t], masked_p[1, :, 256 + 64 * t:320 + 64 * t]],
            axis=1)
        for t in range(2)
    ]).reshape(2, STEPS, 2, ROWS, WIDE)
    result = propagate(masked_h, units, potential, basis).reshape(2, WIDE, WIDE)
    whole = jnp.stack([
        jnp.concatenate(
            [result[0, :, t * BLK:(t + 1) * BLK], result[1, :, t * BLK:(t + 1) * BLK],
             result[0, :, 256 + 64 * t:320 + 64 * t], result[1, :, 256 + 64 * t:320 + 64 * t]],
            axis=1)
        for t in range(2)
    ])
    whole = whole.reshape(2, 3, BLK, 3, BLK) * ppattern[None, :, None, :, None].astype(jnp.bfloat16)
    return whole.reshape(2, WIDE, WIDE)


def solution(mesh):
    in_specs = (
        P("row", "col", None),
        P("row", "col", None, None),
        P("row", "col"),
        P(None, "row", "col"),
        P(),
        P(),
    )
    out_specs = P(None, "row", "col")
    return jax.shard_map(shards, mesh=mesh, in_specs=in_specs, out_specs=out_specs, check_vma=False)
```

```python
import functools
import heapq

import jax
import jax.numpy as jnp
from jax import lax
from jax.experimental import pallas as pl
from jax.experimental.pallas import tpu as pltpu
from jax.sharding import PartitionSpec as P

BLK = 128
KAPPA = 0.4
TIME_STEP = 0.5
MESH = pl.DeviceIdType.MESH

STEPS = 3
ROWS = 64
CHUNKS = ((0, 0, 64, 16), (1, 0, 64, 32), (2, 0, 32, 16), (2, 32, 32, 0))
WIDE = 384


LANES = ((0, 2 * BLK), (2 * BLK, BLK), (0, WIDE))


def groups(s):
    return (1, 0) if s == len(CHUNKS) - 1 else (2,)


def plus_hops(s):
    return 4 if s % 2 == 0 else 3


def antipode_plus(dz):
    return dz % 2 == 0


def messages():
    out = {}
    for s in range(STEPS):
        out["Hm", s] = ("m", 48, [], ("H", s))
    for s, (_, _, rows, y_first) in enumerate(CHUNKS):
        a_kb, b_kb = y_first * 1.5, (rows - y_first) * 1.5
        up, down = plus_hops(s), 7 - plus_hops(s)
        for t in range(1, up + 1):
            out["bz+", s, t] = ("z+", b_kb, [("b", s, 0, 1 - t)], ("b", s, 0, -t))
        for t in range(1, down + 1):
            out["bz-", s, t] = ("z-", b_kb, [("b", s, 0, t - 1)], ("b", s, 0, t))
        for dz in range(-up, down + 1):
            out["by+", s, dz] = ("y+", b_kb, [("b", s, 0, dz)], ("b", s, -1, dz))
            out["by-", s, dz] = ("y-", b_kb, [("b", s, 0, dz)], ("b", s, 1, dz))
            if antipode_plus(dz):
                out["by2", s, dz] = ("y+", b_kb, [("b", s, -1, dz)], ("b", s, 2, dz))
            else:
                out["by2", s, dz] = ("y-", b_kb, [("b", s, 1, dz)], ("b", s, 2, dz))
        if not y_first:
            continue
        out["ay+", s] = ("y+", a_kb, [("a", s, 0)], ("a", s, -1))
        out["ay-", s] = ("y-", a_kb, [("a", s, 0)], ("a", s, 1))
        if s % 2 == 0:
            out["ay2", s] = ("y+", a_kb, [("a", s, -1)], ("a", s, 2))
        else:
            out["ay2", s] = ("y-", a_kb, [("a", s, 1)], ("a", s, 2))
        whole = [("a", s, 0), ("a", s, -1), ("a", s, 1), ("a", s, 2)]
        for t in range(1, up + 1):
            needs = whole if t == 1 else [("A4", s, 1 - t)]
            out["az+", s, t] = ("z+", 4 * a_kb, needs, ("A4", s, -t))
        for t in range(1, down + 1):
            needs = whole if t == 1 else [("A4", s, t - 1)]
            out["az-", s, t] = ("z-", 4 * a_kb, needs, ("A4", s, t))
    for rb in range(4):
        out["Px+", rb] = ("x+", 144, [("P", 0, rb)], ("P", -1, rb))
        out["Px-", rb] = ("x-", 144, [("P", 0, rb)], ("P", 1, rb))
        if rb < 2:
            out["Px2", rb] = ("x+", 144, [("P", -1, rb)], ("P", 2, rb))
        else:
            out["Px2", rb] = ("x-", 144, [("P", 1, rb)], ("P", 2, rb))
        for dx in (0, -1, 1, 2):
            out["Pm", dx, rb] = ("m", 144, [("P", dx, rb)], ("Pm", dx, rb))
    for s, (_, _, rows, _) in enumerate(CHUNKS):
        for g in groups(s):
            kb = rows * 1.5 * LANES[g][1] / WIDE
            for e in (0, 1):
                out["Fx+", s, e, g] = ("x+", kb, [("F", 0, s)], ("F", -1, s, e, g))
                out["Fx-", s, 1 - e, g] = ("x-", kb, [("F", 0, s)], ("F", 1, s, 1 - e, g))
            out["F2+", s, 0, g] = ("x+", kb, [("F", -1, s, 0, g)], ("F", 2, s, 0, g))
            out["F2-", s, 1, g] = ("x-", kb, [("F", 1, s, 1, g)], ("F", 2, s, 1, g))
            out["Fm", 0, s, 2, g] = ("m", 2 * kb, [("F", 0, s)], ("Fm", 0, s, g))
            for dx in (-1, 1, 2):
                for e in (0, 1):
                    out["Fm", dx, s, e, g] = ("m", kb, [("F", dx, s, e, g)],
                                              ("Fm", dx, s, e, g))
    out["Dm",] = ("m", 96, [("I", i) for i in range(4)], ("Dm",))
    for j in range(1, 4):
        out["Dr", j] = ("y-" if j == 3 else "y+", 12 if j != 2 else 24, [("Dc",)], ("Dr", j))
    for k in (1, -1, 2, -2, 3, -3, 4):
        out["Dz", k] = ("z+" if k > 0 else "z-", 12 * abs(k), [("Dl",)], ("Dz", k))
    for j in range(1, 4):
        out["Dy", j] = ("y-" if j == 3 else "y+", 48 if j != 2 else 96, [("Df",)], ("Dy", j))
    return out


def tasks():
    out = {}
    for s in range(STEPS):
        gives = [(k, i, 0, 0) if k == "b" else (k, i, 0)
                 for i, chunk in enumerate(CHUNKS) if chunk[0] == s for k in "ba"]
        out["Hready", s] = (0.05, [("H", s)], gives)
    every_p = [("P", dx, rb) for dx in (0, -1, 1, 2) for rb in range(4)]
    every_p += [("Pm", dx, rb) for dx in (0, -1, 1, 2) for rb in range(4)]
    every_d = [("Dy", i) for i in (1, 2, 3)] + [("Df",)]
    for s, (_, _, rows, y_first) in enumerate(CHUNKS):
        up, down = plus_hops(s), 7 - plus_hops(s)
        near = [("b", s, dy, dz) for dy in (0, -1, 1) for dz in range(-up, down + 1)]
        if y_first:
            near += [("A4", s, dz) for dz in range(-up, down + 1) if dz] + [("a", s, 2)]
        far = [("b", s, 2, dz) for dz in range(-up, down + 1)]
        out["C1", s, 0] = (0.2 + 0.035 * rows, near + every_p, [("C1", s, 0)])
        out["C1", s, 1] = (0.1 + 0.011 * rows, far + [("C1", s, 0)], [("C1", s, 1)])
        out["Ff", s] = (0.5, [("C1", s, 1)] + every_d, [("F", 0, s)])
    out["E",] = (0.5, [("halo",)], [("E",)])
    for i in range(4):
        out["I", i] = (1.5, [("E",)], [("I", i)])
    out["Dc",] = (0.2, [("Dm",)], [("Dc",)])
    out["Dl",] = (0.2, [("Dc",)] + [("Dr", j) for j in (1, 2, 3)], [("Dl",)])
    out["Df",] = (0.2, [("Dl",)] + [("Dz", k) for k in (1, -1, 2, -2, 3, -3, 4)], [("Df",)])
    all_a = [("C1", s, 1) for s in range(len(CHUNKS))]
    def first_of(t, dx, g):
        got = []
        for s, chunk in enumerate(CHUNKS):
            if chunk[0] == t:
                for h in groups(s) if g == 2 else (g,) if g in groups(s) else (2,):
                    if dx == 0:
                        got += [("F", 0, s), ("Fm", 0, s, h)]
                    else:
                        got += [(k, dx, s, e, h) for k in ("F", "Fm") for e in (0, 1)]
        return got

    for t in range(STEPS - 1):
        early = [("C1", 0, 1), ("C1", 1, 1)]
        early += sum([first_of(t, dx, 2) for dx in (0, -1, 1, 2)], [])
        out["S", t, 9, 0, 2, 2] = (2.2, early, [("S", t, 0)])
        out["S", t, 9, 2, 3, 2] = (1.1, early + all_a, [("S", t, 1)])
    gone = [("S", t, i) for t in range(STEPS - 1) for i in (0, 1)]
    t = STEPS - 1
    for g in (1, 0):
        for dx in (0, -1, 1, 2):
            out["S", t, dx, 0, 3, g] = (0.5, all_a + first_of(t, dx, g), [("S", t, dx, g)])
        out["R", g] = (0.6, gone + [("S", t, dx, g) for dx in (0, -1, 1, 2)], [("R", g)])
    return out


RATE = {"m": 200.0}
LINK_RATE = 42.0
BACKLOG = 4.0
D_WAIT = {"Dr": 5.0, "Dz": 6.0, "Dy": 5.0}


def rank_of(name):
    kind = name[0]
    if kind in ("Hm", "Dm", "Dr", "Dy", "Dz"):
        return (-1, 0)
    if kind[0] in "PF":
        return (0, 0)
    return (name[1], 0 if kind in ("bz+", "bz-", "ay+", "ay-", "ay2") else 1)


def schedule():
    every, work = messages(), tasks()
    given_by = {m[3]: n for n, m in every.items()}
    have, sent, done = set(), set(), set()
    free = {}
    arrivals = []
    order = []
    now = 0.0
    free["z+"] = free["z-"] = 2 * 144 / LINK_RATE
    for rb in range(4):
        heapq.heappush(arrivals, (20.0 + rb, 0, ("P0", rb)))
    heapq.heappush(arrivals, (4.0, 0, ("halo",)))
    count = 0

    def issue():
        nonlocal count
        ready = [n for n, m in every.items() if n not in sent and all(d in have for d in m[2])]
        ready.sort(key=rank_of)
        for name in ready:
            link, size, _, _ = every[name]
            start = max(now, free.get(link, 0.0))
            if start - now > BACKLOG and link != "m" and name[0][0] != "D":
                continue
            end = start + size / RATE.get(link, LINK_RATE)
            free[link] = end
            sent.add(name)
            count += 1
            wait = D_WAIT.get(name[0], 1.0 if link == "m" else 1.8)
            heapq.heappush(arrivals, (end + wait, count, name))
            order.append(("send", name))

    while len(done) < len(work) or arrivals:
        issue()
        if arrivals and arrivals[0][0] <= now:
            _, _, name = heapq.heappop(arrivals)
            order.append(("wait", name))
            if name[0] == "P0":
                have.add(("P", 0, name[1]))
            elif name[0] == "halo":
                have.add(name)
            else:
                have.add(every[name][3])
            continue
        ready = [n for n, w in work.items() if n not in done and all(d in have for d in w[1])]
        if ready:
            name = ready[0]
            now += work[name][0]
            done.add(name)
            have.update(work[name][2])
            order.append(("work", name))
            continue
        later = [arrivals[0][0]] if arrivals else []
        waiting = [n for n, m in every.items() if n not in sent and all(d in have for d in m[2])]
        later += [free[every[n][0]] - BACKLOG + 0.01 for n in waiting]
        now = max(now + 0.01, min(later))
    return order, now


def core_kernel(order, ham_ref, den_ref, pot_ref, basis_ref, hmask_ref, pmask_ref, out_ref, a_buf, b_buf, f_buf, o_buf,
                f_acc, s_acc, d_mate, d_chip, d_all, d_got, d_line,
                basis_buf, halo, eff, part, h_ref, p_ref,
                send_sem, recv_sem, local_sem, pin_sem, pin_send, ret_sem, ret_send,
                halo_sem, halo_send, basis_sem):
    row, col = lax.axis_index("row"), lax.axis_index("col")
    x, zl = row // 4, row % 4
    y, zh, c = col // 4, (col // 2) % 2, col % 2
    z = zh * 4 + zl
    basis_copy = pltpu.make_async_copy(basis_ref, basis_buf, basis_sem)
    basis_copy.start()

    def dev(dx=0, dy=0, dz=0, core=None):
        zz = (z + dz) % 8
        core = c if core is None else core
        return (((x + dx) % 4) * 4 + zz % 4, ((y + dy) % 4) * 4 + (zz // 4) * 2 + core)

    def dev_line(q, core):
        return (x * 4 + q, y * 4 + zh * 2 + core)

    barrier = pltpu.get_barrier_semaphore()
    friends = [dev(core=1 - c), dev(dx=1), dev(dx=-1)]
    friends += [dev(dy=j) for j in (1, 2, 3)] + [dev(dz=j) for j in range(1, 8)]
    friends += [dev(dy=j, dz=4) for j in (1, 2, 3)]
    friends += [dev_line((zl + j) % 4, 1 - c) for j in (1, 2, 3)]
    beside = [((row + 1) % 16, col), ((row + 15) % 16, col), (row, (col + 1) % 16),
              (row, (col + 15) % 16)]
    friends += beside
    for friend in friends:
        pl.semaphore_signal(barrier, inc=1, device_id=friend, device_id_type=MESH)
    for t in range(3):
        for j in range(3):
            keep = hmask_ref[row * 3 + t, col * 3 + j].astype(jnp.float32)
            tile = ham_ref[t * BLK:(t + 1) * BLK, j * BLK:(j + 1) * BLK].astype(jnp.float32) * keep
            h_ref[t, :, :, j * BLK:(j + 1) * BLK] = (
                tile.astype(jnp.bfloat16).reshape(2, ROWS, BLK))
    pl.semaphore_wait(barrier, len(friends))

    names = list(messages())
    index = {n: i for i, n in enumerate(names)}

    def block(s, dy, dz, color):
        zz = (z + dz) % 8
        tile, first, count, y_first = CHUNKS[s]
        rows = pl.ds(first, y_first) if color == "a" else pl.ds(first + y_first, count - y_first)
        return a_buf.at[tile, (y + dy) % 4, zz // 4, zz % 4, rows]

    def block4(s, dz):
        zz = (z + dz) % 8
        tile, first, _, y_first = CHUNKS[s]
        return a_buf.at[tile, :, zz // 4, zz % 4, pl.ds(first, y_first)]

    def lanes(core):
        return pl.ds(pl.multiple_of(core * WIDE, 128), WIDE)

    def b_slot(dx, rb, core):
        return b_buf.at[(x + dx) % 4, rb, :, core]

    def f_slot(dx, s, core, rbs, g):
        tile, first, count, _ = CHUNKS[s]
        return f_buf.at[(x + dx) % 4, rbs, tile, core, pl.ds(first, count), pl.ds(*LANES[g])]

    FULL, LOW, HIGH = pl.ds(0, 4), pl.ds(0, 2), pl.ds(2, 2)
    PAIR = (LOW, HIGH, FULL)

    def ends(name):
        kind = name[0]
        if kind == "Hm":
            s = name[1]
            return (h_ref.at[s, 1 - c], a_buf.at[s, y, zh, zl, :, lanes(c)],
                    a_buf.at[s, y, zh, zl, :, lanes(1 - c)], dev(core=1 - c))
        if kind == "bz+":
            _, s, t = name
            src = block(s, 0, 1 - t, "b")
            return src, src, block(s, 0, -t, "b"), dev(dz=1)
        if kind == "bz-":
            _, s, t = name
            src = block(s, 0, t - 1, "b")
            return src, src, block(s, 0, t, "b"), dev(dz=-1)
        if kind == "by+":
            _, s, dz = name
            src = block(s, 0, dz, "b")
            return src, src, block(s, -1, dz, "b"), dev(dy=1)
        if kind == "by-":
            _, s, dz = name
            src = block(s, 0, dz, "b")
            return src, src, block(s, 1, dz, "b"), dev(dy=-1)
        if kind == "by2":
            _, s, dz = name
            way = 1 if antipode_plus(dz) else -1
            src = block(s, -way, dz, "b")
            return src, src, block(s, 2, dz, "b"), dev(dy=way)
        if kind == "ay+":
            src = block(name[1], 0, 0, "a")
            return src, src, block(name[1], -1, 0, "a"), dev(dy=1)
        if kind == "ay-":
            src = block(name[1], 0, 0, "a")
            return src, src, block(name[1], 1, 0, "a"), dev(dy=-1)
        if kind == "ay2":
            way = 1 if name[1] % 2 == 0 else -1
            src = block(name[1], -way, 0, "a")
            return src, src, block(name[1], 2, 0, "a"), dev(dy=way)
        if kind == "az+":
            _, s, t = name
            src = block4(s, 1 - t)
            return src, src, block4(s, -t), dev(dz=1)
        if kind == "az-":
            _, s, t = name
            src = block4(s, t - 1)
            return src, src, block4(s, t), dev(dz=-1)
        if kind == "Px+":
            src = b_slot(0, name[1], c)
            return src, src, b_slot(-1, name[1], c), dev(dx=1)
        if kind == "Px-":
            src = b_slot(0, name[1], c)
            return src, src, b_slot(1, name[1], c), dev(dx=-1)
        if kind == "Px2":
            way = 1 if name[1] < 2 else -1
            src = b_slot(-way, name[1], c)
            return src, src, b_slot(2, name[1], c), dev(dx=way)
        if kind == "Pm":
            _, dx, rb = name
            src = b_slot(dx, rb, c)
            return src, src, b_slot(dx, rb, 1 - c), dev(core=1 - c)
        if kind in ("Fx+", "Fx-", "F2+", "F2-"):
            _, s, e, g = name
            way = 1 if kind[2] == "+" else -1
            frm, to = (0, -way) if kind[1] == "x" else (-way, 2)
            src = f_slot(frm, s, c, PAIR[e], g)
            return src, src, f_slot(to, s, c, PAIR[e], g), dev(dx=way)
        if kind == "Fm":
            _, dx, s, e, g = name
            src = f_slot(dx, s, c, PAIR[e], g)
            return src, src, f_slot(dx, s, 1 - c, PAIR[e], g), dev(core=1 - c)
        if kind == "Dm":
            return part.at[:, 1 - c], d_mate, d_mate, dev(core=1 - c)
        if kind == "Dr":
            j = name[1]
            return d_chip.at[(y + j) % 4], d_got.at[j - 1], d_got.at[j - 1], dev(dy=j)
        if kind == "Dz":
            k = name[1]
            zz = (z - k) % 8
            src = d_line.at[zh, zl]
            return src, src, d_line.at[zz // 4, zz % 4], dev(dz=k)
        if kind == "Dy":
            j = name[1]
            src = d_all.at[:, y]
            return src, src, d_all.at[:, (y - j) % 4], dev(dy=j)
        raise KeyError(name)

    def outgoing(name):
        src, dst, _, target = ends(name)
        i = index[name]
        return pltpu.make_async_remote_copy(
            src_ref=src, dst_ref=dst, send_sem=send_sem.at[i], recv_sem=recv_sem.at[i],
            device_id=target, device_id_type=MESH)

    def incoming(name):
        src, _, land, target = ends(name)
        i = index[name]
        return pltpu.make_async_remote_copy(
            src_ref=land, dst_ref=land, send_sem=send_sem.at[i], recv_sem=recv_sem.at[i],
            device_id=target, device_id_type=MESH)

    to_side = [row < 15, row > 0, col < 15, col > 0]
    from_side = [row > 0, row < 15, col > 0, col < 15]

    def halo_copy(i):
        return pltpu.make_async_remote_copy(
            src_ref=pot_ref, dst_ref=halo.at[i], send_sem=halo_send.at[i],
            recv_sem=halo_sem.at[i], device_id=beside[i], device_id_type=MESH)

    for i in range(4):
        @pl.when(to_side[i])
        def _():
            halo_copy(i).start()

    def wait_halo():
        for i in range(4):
            @pl.when(from_side[i])
            def _():
                halo_copy(i).wait_recv()

            @pl.when(jnp.logical_not(from_side[i]))
            def _():
                halo[i] = jnp.zeros((2, 4, 512), jnp.float32)

    own = [pltpu.make_async_copy(h_ref.at[s, c], a_buf.at[s, y, zh, zl, :, lanes(c)],
                                 local_sem.at[s]) for s in range(STEPS)]
    for copy in own:
        copy.start()

    def p_copy(hf, r):
        q = 2 * c + hf
        src = p_ref.at[hf, :, r]
        here = (q == zl) & (r == c)
        dst = b_buf.at[x, zl, :, r]

        def local():
            return pltpu.make_async_copy(src, dst, pin_sem.at[zl])

        def remote():
            return pltpu.make_async_remote_copy(
                src_ref=src, dst_ref=dst, send_sem=pin_send.at[hf, r], recv_sem=pin_sem.at[zl],
                device_id=dev_line(q, r), device_id_type=MESH)

        return here, local, remote

    def pack_p():
        lane = lax.broadcasted_iota(jnp.int32, (BLK, BLK), 1)

        def put(hf, t, j, value):
            p_ref[hf, t, :, :, j * BLK:(j + 1) * BLK] = (
                value.astype(jnp.bfloat16).reshape(2, ROWS, BLK))

        for t in range(3):
            tiles = []
            for j in range(3):
                keep = pmask_ref[row * 3 + t, col * 3 + j].astype(jnp.float32)
                tiles.append([
                    den_ref[p, t * BLK:(t + 1) * BLK, j * BLK:(j + 1) * BLK].astype(jnp.float32)
                    * keep for p in range(2)])
            for j in range(2):
                for p in range(2):
                    put(j, t, p, tiles[j][p])
            turned = [pltpu.roll(v, BLK // 2, 1) for v in tiles[2]]
            put(0, t, 2, jnp.where(lane < BLK // 2, tiles[2][0], turned[1]))
            put(1, t, 2, jnp.where(lane < BLK // 2, turned[0], tiles[2][1]))

    def start_p():
        for hf in range(2):
            for r in range(2):
                here, local, remote = p_copy(hf, r)

                @pl.when(here)
                def _():
                    local().start()

                @pl.when(jnp.logical_not(here))
                def _():
                    remote().start()

    def first_product(s, far):
        tile, first, count, _ = CHUNKS[s]
        rows = slice(first, first + count)
        if not far:
            f_acc[tile, :, rows] = jnp.zeros((4, count, WIDE), jnp.float32)

        def body(k, carry):
            yy, zz = (y + (k // 2) + 3) % 4, k % 2
            left = a_buf[tile, yy, zz, :, rows].reshape(4 * count, 2 * WIDE)
            right = b_buf[yy, pl.ds(zz * 2, 2)].reshape(2 * WIDE, WIDE)
            more = jnp.dot(left, right, preferred_element_type=jnp.float32)
            f_acc[tile, :, rows] += more.reshape(4, count, WIDE)
            return carry

        lax.fori_loop(6 if far else 0, 8 if far else 6, body, 0)

    def diagonal(rb, s):
        return d_all[rb].astype(jnp.float32).reshape(STEPS, ROWS, BLK)[s].astype(jnp.bfloat16)

    def first_finish(s):
        tile, first, count, _ = CHUNKS[s]
        rows = slice(first, first + count)
        for rb in range(4):
            right = b_buf[x, rb, tile].reshape(BLK, WIDE)
            total = f_acc[tile, rb, rows] + jnp.dot(diagonal(rb, tile)[rows], right,
                                                    preferred_element_type=jnp.float32)
            f_acc[tile, rb, rows] = total
            f_buf[x, rb, tile, c, rows] = total.astype(jnp.bfloat16)

    def second_product(s, dx, low, high, g):
        lane = slice(LANES[g][0], sum(LANES[g]))
        cuts = [slice(e * WIDE + s * BLK, e * WIDE + (s + 1) * BLK) for e in range(2)]

        def body(k, carry):
            xx, t = (x + (k // (high - low) if dx == 9 else dx)) % 4, low + k % (high - low)
            left = jnp.concatenate(
                [a_buf[t, xx, zz, :, :, cut].reshape(4 * ROWS, BLK)
                 for zz in range(2) for cut in cuts], axis=1)
            right = f_buf[xx, :, s, :, :, lane].reshape(4 * BLK, LANES[g][1])
            more = jnp.dot(left, right, preferred_element_type=jnp.float32)
            s_acc[t, :, :, lane] += more.reshape(4, ROWS, LANES[g][1])
            return carry

        lax.fori_loop(0, (4 if dx == 9 else 1) * (high - low), body, 0)
        if dx in (0, 9) and low <= s < high:
            for rb in range(4):
                right = f_buf[x, rb, s, :, :, lane].reshape(BLK, LANES[g][1])
                s_acc[s, rb, :, lane] += jnp.dot(diagonal(rb, s), right,
                                                 preferred_element_type=jnp.float32)

    def screen():
        wait_halo()
        zero = jnp.zeros((1, 1), jnp.float32)
        for i in range(2):
            for j in range(4):
                here = pot_ref[i, j:j + 1]
                below = pot_ref[0, j:j + 1] if i else halo[0, 1, j:j + 1]
                above = halo[1, 0, j:j + 1] if i else pot_ref[1, j:j + 1]
                left = pot_ref[i, j - 1:j] if j else halo[2, i, 3:4]
                right = pot_ref[i, j + 1:j + 2] if j < 3 else halo[3, i, 0:1]
                later = jnp.concatenate([here[:, 1:], zero], axis=1)
                earlier = jnp.concatenate([zero, here[:, :-1]], axis=1)
                total = above + below
                total = total + right + left
                total = total + later + earlier
                eff[i, j:j + 1] = here + KAPPA * (total - 6.0 * here)

    def integrate(i):
        if i == 0:
            basis_copy.wait()
            part[...] = jnp.zeros_like(part)

        def body(j, carry):
            cell = 2 * i + j
            table = basis_buf[cell // 4, cell % 4]
            scale = eff[cell // 4, pl.ds(cell % 4, 1)]
            weighted = (table.astype(jnp.float32) * scale).astype(jnp.bfloat16)
            for k in range(3):
                rows = slice(k * BLK, (k + 1) * BLK)
                more = lax.dot_general(weighted[rows], table[rows], (((1,), (1,)), ((), ())),
                                       preferred_element_type=jnp.float32)
                part[k] += more.reshape(2, ROWS, BLK)
            return carry

        lax.fori_loop(0, 2, body, 0)

    def line_integrals():
        total = d_chip[y].astype(jnp.float32)
        for j in range(3):
            total = total + d_got[j].astype(jnp.float32)
        d_line[zh, zl] = total.astype(jnp.bfloat16)

    def finish_integrals():
        factor = float(BLK * 2 * 64 * 512) ** -0.5
        total = d_line[0].astype(jnp.float32) + d_line[1].astype(jnp.float32)
        d_all[:, y] = (total * factor).astype(jnp.bfloat16)

    lane_of = lax.broadcasted_iota(jnp.int32, (ROWS, BLK), 1)
    quarter = 0.5 * TIME_STEP * TIME_STEP
    targets = [(zl // 2) * 2 + 1 - zl % 2, 3 - zl, (zl + 2) % 4, zl]

    def back(k, g):
        lane = pl.ds(*LANES[g])
        src = o_buf.at[k, :, :, lane]
        dst = out_ref.at[zl % 2, :, c, :, lane]

        def local():
            return pltpu.make_async_copy(src, dst, ret_sem.at[zl % 2, c, g])

        def remote():
            return pltpu.make_async_remote_copy(
                src_ref=src, dst_ref=dst, send_sem=ret_send.at[k, g],
                recv_sem=ret_sem.at[zl % 2, c, g],
                device_id=dev_line(targets[k], zl // 2), device_id_type=MESH)

        return zl // 2 == c, local, remote

    def give_back(g):
        for k in (1, 2, 0, 3):
            rb = targets[k]
            for s in range(STEPS):
                f = f_acc[s, rb]
                if g:
                    turned = pltpu.roll(f[:, 2 * BLK:], BLK // 2, 1)
                    turn = jnp.where(lane_of < BLK // 2, turned, -turned)
                else:
                    turn = jnp.concatenate([f[:, BLK:2 * BLK], -f[:, :BLK]], axis=1)
                cut = slice(LANES[g][0], sum(LANES[g]))
                base = b_buf[x, rb, s, c, :, cut].astype(jnp.float32)
                o_buf[k, s, :, cut] = (
                    base + TIME_STEP * turn - quarter * s_acc[s, rb, :, cut]
                ).astype(jnp.bfloat16)
            here, local, remote = back(k, g)
            if k < 3:
                remote().start()
                continue

            @pl.when(here)
            def _():
                local().start()

            @pl.when(jnp.logical_not(here))
            def _():
                remote().start()

    def run(name):
        kind = name[0]
        if kind == "Hready":
            own[name[1]].wait()
        elif kind == "E":
            screen()
        elif kind == "I":
            integrate(name[1])
        elif kind == "C1":
            first_product(name[1], name[2])
        elif kind == "Ff":
            first_finish(name[1])
        elif kind == "S":
            second_product(*name[1:])
        elif kind == "R":
            give_back(name[1])
        elif kind == "Dc":
            d_chip[...] = (part[:, c] + d_mate[...]).reshape(4, 48, BLK).astype(jnp.bfloat16)
        elif kind == "Dl":
            line_integrals()
        elif kind == "Df":
            finish_integrals()

    opened = False
    for what, name in order:
        if what != "send" and not opened:
            opened = True
            pack_p()
            start_p()
            s_acc[...] = jnp.zeros_like(s_acc)
        if what == "send":
            outgoing(name).start()
        elif what == "wait":
            if name[0] == "halo":
                continue
            if name[0] == "P0":
                rb = name[1]
                land = b_buf.at[x, rb, :, c]
                pltpu.make_async_copy(land, land, pin_sem.at[rb]).wait()
            else:
                incoming(name).wait_recv()
        else:
            run(name)

    for g in range(2):
        for hf in range(2):
            for r in range(2):
                land = out_ref.at[hf, :, r, :, pl.ds(*LANES[g])]
                pltpu.make_async_copy(land, land, ret_sem.at[hf, r, g]).wait()

    for what, name in order:
        if what == "send":
            outgoing(name).wait_send()
    for hf in range(2):
        for r in range(2):
            here, _, remote = p_copy(hf, r)

            @pl.when(jnp.logical_not(here))
            def _():
                remote().wait_send()
    for g in range(2):
        for k in range(3):
            back(k, g)[2]().wait_send()
        here, _, remote = back(3, g)

        @pl.when(jnp.logical_not(here))
        def _():
            remote().wait_send()
    for i in range(4):
        @pl.when(to_side[i])
        def _():
            halo_copy(i).wait_send()


def propagate(h, p, potential, basis, hmask, pmask):
    order, _ = schedule()
    total = len(messages())
    bf, f32 = jnp.bfloat16, jnp.float32
    any_space = pl.BlockSpec(memory_space=pl.ANY)
    vmem = pl.BlockSpec(memory_space=pltpu.VMEM)
    smem = pl.BlockSpec(memory_space=pltpu.SMEM)
    return pl.pallas_call(
        functools.partial(core_kernel, order),
        out_shape=jax.ShapeDtypeStruct((2, STEPS, 2, ROWS, WIDE), bf),
        in_specs=[vmem, vmem, vmem, any_space, smem, smem],
        out_specs=any_space,
        scratch_shapes=[
            pltpu.VMEM((STEPS, 4, 2, 4, ROWS, 2 * WIDE), bf),
            pltpu.VMEM((4, 4, STEPS, 2, ROWS, WIDE), bf),
            pltpu.VMEM((4, 4, STEPS, 2, ROWS, WIDE), bf),
            pltpu.VMEM((4, STEPS, ROWS, WIDE), bf),
            pltpu.VMEM((STEPS, 4, ROWS, WIDE), f32),
            pltpu.VMEM((STEPS, 4, ROWS, WIDE), f32),
            pltpu.VMEM((STEPS, ROWS, BLK), f32),
            pltpu.VMEM((4, 48, BLK), bf),
            pltpu.VMEM((4, 4, 48, BLK), bf),
            pltpu.VMEM((3, 48, BLK), bf),
            pltpu.VMEM((2, 4, 48, BLK), bf),
            pltpu.VMEM((2, 4, WIDE, 512), bf),
            pltpu.VMEM((4, 2, 4, 512), f32),
            pltpu.VMEM((2, 4, 512), f32),
            pltpu.VMEM((STEPS, 2, ROWS, BLK), f32),
            pltpu.VMEM((STEPS, 2, ROWS, WIDE), bf),
            pltpu.VMEM((2, STEPS, 2, ROWS, WIDE), bf),
            pltpu.SemaphoreType.DMA((total,)),
            pltpu.SemaphoreType.DMA((total,)),
            pltpu.SemaphoreType.DMA((STEPS,)),
            pltpu.SemaphoreType.DMA((4,)),
            pltpu.SemaphoreType.DMA((2, 2)),
            pltpu.SemaphoreType.DMA((2, 2, 2)),
            pltpu.SemaphoreType.DMA((4, 2)),
            pltpu.SemaphoreType.DMA((4,)),
            pltpu.SemaphoreType.DMA((4,)),
            pltpu.SemaphoreType.DMA,
        ],
        compiler_params=pltpu.CompilerParams(
            collective_id=0, has_side_effects=True, vmem_limit_bytes=60 << 20),
        name="propagate",
    )(h, p, potential, basis, hmask, pmask)


def shards(potential, basis, hamiltonian, density, hmask, pmask):
    row_start = lax.axis_index("row") * 3
    col_start = lax.axis_index("col") * 3
    ppattern = lax.dynamic_slice(pmask, (row_start, col_start), (3, 3))
    result = propagate(hamiltonian, density, potential, basis, hmask, pmask).reshape(2, WIDE, WIDE)
    whole = jnp.stack([
        jnp.concatenate(
            [result[0, :, t * BLK:(t + 1) * BLK], result[1, :, t * BLK:(t + 1) * BLK],
             result[0, :, 256 + 64 * t:320 + 64 * t], result[1, :, 256 + 64 * t:320 + 64 * t]],
            axis=1)
        for t in range(2)
    ])
    whole = whole.reshape(2, 3, BLK, 3, BLK) * ppattern[None, :, None, :, None].astype(jnp.bfloat16)
    return whole.reshape(2, WIDE, WIDE)


def solution(mesh):
    in_specs = (
        P("row", "col", None),
        P("row", "col", None, None),
        P("row", "col"),
        P(None, "row", "col"),
        P(),
        P(),
    )
    out_specs = P(None, "row", "col")
    return jax.shard_map(shards, mesh=mesh, in_specs=in_specs, out_specs=out_specs, check_vma=False)
```

```python
import functools
import heapq

import jax
import jax.numpy as jnp
from jax import lax
from jax.experimental import pallas as pl
from jax.experimental.pallas import tpu as pltpu
from jax.sharding import PartitionSpec as P

BLK = 128
KAPPA = 0.4
TIME_STEP = 0.5
MESH = pl.DeviceIdType.MESH

STEPS = 3
ROWS = 64
CHUNKS = ((0, 0, 64, 16), (1, 0, 64, 32), (2, 0, 32, 16), (2, 32, 32, 0))
WIDE = 384


LANES = ((0, 2 * BLK), (2 * BLK, BLK), (0, WIDE))


def groups(s):
    return (1, 0) if s == len(CHUNKS) - 1 else (2,)


def plus_hops(s):
    return 4 if s % 2 == 0 else 3


def antipode_plus(dz):
    return dz % 2 == 0


def messages():
    out = {}
    for s in range(STEPS):
        out["Hm", s] = ("m", 48, [], ("H", s))
    for s, (_, _, rows, y_first) in enumerate(CHUNKS):
        a_kb, b_kb = y_first * 1.5, (rows - y_first) * 1.5
        up, down = plus_hops(s), 7 - plus_hops(s)
        for t in range(1, up + 1):
            out["bz+", s, t] = ("z+", b_kb, [("b", s, 0, 1 - t)], ("b", s, 0, -t))
        for t in range(1, down + 1):
            out["bz-", s, t] = ("z-", b_kb, [("b", s, 0, t - 1)], ("b", s, 0, t))
        for dz in range(-up, down + 1):
            out["by+", s, dz] = ("y+", b_kb, [("b", s, 0, dz)], ("b", s, -1, dz))
            out["by-", s, dz] = ("y-", b_kb, [("b", s, 0, dz)], ("b", s, 1, dz))
            if antipode_plus(dz):
                out["by2", s, dz] = ("y+", b_kb, [("b", s, -1, dz)], ("b", s, 2, dz))
            else:
                out["by2", s, dz] = ("y-", b_kb, [("b", s, 1, dz)], ("b", s, 2, dz))
        if not y_first:
            continue
        out["ay+", s] = ("y+", a_kb, [("a", s, 0)], ("a", s, -1))
        out["ay-", s] = ("y-", a_kb, [("a", s, 0)], ("a", s, 1))
        if s % 2 == 0:
            out["ay2", s] = ("y+", a_kb, [("a", s, -1)], ("a", s, 2))
        else:
            out["ay2", s] = ("y-", a_kb, [("a", s, 1)], ("a", s, 2))
        whole = [("a", s, 0), ("a", s, -1), ("a", s, 1), ("a", s, 2)]
        for t in range(1, up + 1):
            needs = whole if t == 1 else [("A4", s, 1 - t)]
            out["az+", s, t] = ("z+", 4 * a_kb, needs, ("A4", s, -t))
        for t in range(1, down + 1):
            needs = whole if t == 1 else [("A4", s, t - 1)]
            out["az-", s, t] = ("z-", 4 * a_kb, needs, ("A4", s, t))
    for rb in range(4):
        out["Px+", rb] = ("x+", 144, [("P", 0, rb)], ("P", -1, rb))
        out["Px-", rb] = ("x-", 144, [("P", 0, rb)], ("P", 1, rb))
        if rb < 2:
            out["Px2", rb] = ("x+", 144, [("P", -1, rb)], ("P", 2, rb))
        else:
            out["Px2", rb] = ("x-", 144, [("P", 1, rb)], ("P", 2, rb))
        for dx in (0, -1, 1, 2):
            out["Pm", dx, rb] = ("m", 144, [("P", dx, rb)], ("Pm", dx, rb))
    for s, (_, _, rows, _) in enumerate(CHUNKS):
        for g in groups(s):
            kb = rows * 1.5 * LANES[g][1] / WIDE
            for e in (0, 1):
                out["Fx+", s, e, g] = ("x+", kb, [("F", 0, s)], ("F", -1, s, e, g))
                out["Fx-", s, 1 - e, g] = ("x-", kb, [("F", 0, s)], ("F", 1, s, 1 - e, g))
            out["F2+", s, 0, g] = ("x+", kb, [("F", -1, s, 0, g)], ("F", 2, s, 0, g))
            out["F2-", s, 1, g] = ("x-", kb, [("F", 1, s, 1, g)], ("F", 2, s, 1, g))
            out["Fm", 0, s, 2, g] = ("m", 2 * kb, [("F", 0, s)], ("Fm", 0, s, g))
            for dx in (-1, 1, 2):
                for e in (0, 1):
                    out["Fm", dx, s, e, g] = ("m", kb, [("F", dx, s, e, g)],
                                              ("Fm", dx, s, e, g))
    out["Dm",] = ("m", 96, [("I", i) for i in range(4)], ("Dm",))
    for j in range(1, 4):
        out["Dr", j] = ("y-" if j == 3 else "y+", 12 if j != 2 else 24, [("Dc",)], ("Dr", j))
    for k in (1, -1, 2, -2, 3, -3, 4):
        out["Dz", k] = ("z+" if k > 0 else "z-", 12 * abs(k), [("Dl",)], ("Dz", k))
    for j in range(1, 4):
        out["Dy", j] = ("y-" if j == 3 else "y+", 48 if j != 2 else 96, [("Df",)], ("Dy", j))
    return out


def tasks():
    out = {}
    for s in range(STEPS):
        gives = [(k, i, 0, 0) if k == "b" else (k, i, 0)
                 for i, chunk in enumerate(CHUNKS) if chunk[0] == s for k in "ba"]
        out["Hready", s] = (0.05, [("H", s)], gives)
    every_p = [("P", dx, rb) for dx in (0, -1, 1, 2) for rb in range(4)]
    every_p += [("Pm", dx, rb) for dx in (0, -1, 1, 2) for rb in range(4)]
    every_d = [("Dy", i) for i in (1, 2, 3)] + [("Df",)]
    for s, (_, _, rows, y_first) in enumerate(CHUNKS):
        up, down = plus_hops(s), 7 - plus_hops(s)
        near = [("b", s, dy, dz) for dy in (0, -1, 1) for dz in range(-up, down + 1)]
        if y_first:
            near += [("A4", s, dz) for dz in range(-up, down + 1) if dz] + [("a", s, 2)]
        far = [("b", s, 2, dz) for dz in range(-up, down + 1)]
        out["C1", s, 0] = (0.2 + 0.035 * rows, near + every_p, [("C1", s, 0)])
        out["C1", s, 1] = (0.1 + 0.011 * rows, far + [("C1", s, 0)], [("C1", s, 1)])
        out["Ff", s] = (0.5, [("C1", s, 1)] + every_d, [("F", 0, s)])
    out["E",] = (0.5, [("halo",)], [("E",)])
    for i in range(4):
        out["I", i] = (1.5, [("E",)], [("I", i)])
    out["Dc",] = (0.2, [("Dm",)], [("Dc",)])
    out["Dl",] = (0.2, [("Dc",)] + [("Dr", j) for j in (1, 2, 3)], [("Dl",)])
    out["Df",] = (0.2, [("Dl",)] + [("Dz", k) for k in (1, -1, 2, -2, 3, -3, 4)], [("Df",)])
    all_a = [("C1", s, 1) for s in range(len(CHUNKS))]
    def first_of(t, dx, g):
        got = []
        for s, chunk in enumerate(CHUNKS):
            if chunk[0] == t:
                for h in groups(s) if g == 2 else (g,) if g in groups(s) else (2,):
                    if dx == 0:
                        got += [("F", 0, s), ("Fm", 0, s, h)]
                    else:
                        got += [(k, dx, s, e, h) for k in ("F", "Fm") for e in (0, 1)]
        return got

    for t in range(STEPS - 1):
        early = [("C1", 0, 1), ("C1", 1, 1)]
        early += sum([first_of(t, dx, 2) for dx in (0, -1, 1, 2)], [])
        out["S", t, 9, 0, 2, 2] = (2.2, early, [("S", t, 0)])
        out["S", t, 9, 2, 3, 2] = (1.1, early + all_a, [("S", t, 1)])
    gone = [("S", t, i) for t in range(STEPS - 1) for i in (0, 1)]
    t = STEPS - 1
    for g in (1, 0):
        for dx in (0, -1, 1, 2):
            out["S", t, dx, 0, 3, g] = (0.5, all_a + first_of(t, dx, g), [("S", t, dx, g)])
        out["R", g] = (0.6, gone + [("S", t, dx, g) for dx in (0, -1, 1, 2)], [("R", g)])
    return out


RATE = {"m": 200.0}
LINK_RATE = 42.0
BACKLOG = 4.0
D_WAIT = {"Dr": 5.0, "Dz": 6.0, "Dy": 5.0}


def rank_of(name):
    kind = name[0]
    if kind in ("Hm", "Dm", "Dr", "Dy", "Dz"):
        return (-1, 0)
    if kind[0] in "PF":
        return (0, 0)
    return (name[1], 0 if kind in ("bz+", "bz-", "ay+", "ay-", "ay2") else 1)


def schedule():
    every, work = messages(), tasks()
    given_by = {m[3]: n for n, m in every.items()}
    have, sent, done = set(), set(), set()
    free = {}
    arrivals = []
    order = []
    now = 0.0
    free["z+"] = free["z-"] = 2 * 144 / LINK_RATE
    for rb in range(4):
        heapq.heappush(arrivals, (20.0 + rb, 0, ("P0", rb)))
    heapq.heappush(arrivals, (4.0, 0, ("halo",)))
    count = 0

    def issue():
        nonlocal count
        ready = [n for n, m in every.items() if n not in sent and all(d in have for d in m[2])]
        ready.sort(key=rank_of)
        for name in ready:
            link, size, _, _ = every[name]
            start = max(now, free.get(link, 0.0))
            if start - now > BACKLOG and link != "m" and name[0][0] != "D":
                continue
            end = start + size / RATE.get(link, LINK_RATE)
            free[link] = end
            sent.add(name)
            count += 1
            wait = D_WAIT.get(name[0], 1.0 if link == "m" else 1.8)
            heapq.heappush(arrivals, (end + wait, count, name))
            order.append(("send", name))

    while len(done) < len(work) or arrivals:
        issue()
        if arrivals and arrivals[0][0] <= now:
            _, _, name = heapq.heappop(arrivals)
            order.append(("wait", name))
            if name[0] == "P0":
                have.add(("P", 0, name[1]))
            elif name[0] == "halo":
                have.add(name)
            else:
                have.add(every[name][3])
            continue
        ready = [n for n, w in work.items() if n not in done and all(d in have for d in w[1])]
        if ready:
            name = ready[0]
            now += work[name][0]
            done.add(name)
            have.update(work[name][2])
            order.append(("work", name))
            continue
        later = [arrivals[0][0]] if arrivals else []
        waiting = [n for n, m in every.items() if n not in sent and all(d in have for d in m[2])]
        later += [free[every[n][0]] - BACKLOG + 0.01 for n in waiting]
        now = max(now + 0.01, min(later))
    return order, now


def core_kernel(order, ham_in, den_in, pot_in, basis_ref, hmask_ref, pmask_ref, out_ref, a_buf, b_buf, f_buf, o_buf,
                f_acc, s_acc, d_mate, d_chip, d_all, d_got, d_line,
                basis_buf, halo, eff, part, h_ref, p_ref,
                ham_ref, den_ref, pot_ref, third,
                send_sem, recv_sem, local_sem, pin_sem, pin_send, ret_sem, ret_send,
                halo_sem, halo_send, basis_sem, in_sem, third_sem):
    row, col = lax.axis_index("row"), lax.axis_index("col")
    x, zl = row // 4, row % 4
    y, zh, c = col // 4, (col // 2) % 2, col % 2
    z = zh * 4 + zl
    ham_copy = pltpu.make_async_copy(ham_in, ham_ref, in_sem.at[0])
    pot_copy = pltpu.make_async_copy(pot_in, pot_ref, in_sem.at[1])
    den_copy = pltpu.make_async_copy(den_in, den_ref, in_sem.at[2])
    basis_copy = pltpu.make_async_copy(basis_ref, basis_buf, basis_sem)
    for copy in (ham_copy, pot_copy, den_copy, basis_copy):
        copy.start()

    def dev(dx=0, dy=0, dz=0, core=None):
        zz = (z + dz) % 8
        core = c if core is None else core
        return (((x + dx) % 4) * 4 + zz % 4, ((y + dy) % 4) * 4 + (zz // 4) * 2 + core)

    def dev_line(q, core):
        return (x * 4 + q, y * 4 + zh * 2 + core)

    barrier = pltpu.get_barrier_semaphore()
    friends = [dev(core=1 - c), dev(dx=1), dev(dx=-1)]
    friends += [dev(dy=j) for j in (1, 2, 3)] + [dev(dz=j) for j in range(1, 8)]
    friends += [dev(dy=j, dz=4) for j in (1, 2, 3)]
    friends += [dev_line((zl + j) % 4, 1 - c) for j in (1, 2, 3)]
    beside = [((row + 1) % 16, col), ((row + 15) % 16, col), (row, (col + 1) % 16),
              (row, (col + 15) % 16)]
    friends += beside
    for friend in friends:
        pl.semaphore_signal(barrier, inc=1, device_id=friend, device_id_type=MESH)
    ham_copy.wait()
    for t in range(3):
        for j in range(3):
            keep = hmask_ref[row * 3 + t, col * 3 + j].astype(jnp.float32)
            tile = ham_ref[t * BLK:(t + 1) * BLK, j * BLK:(j + 1) * BLK].astype(jnp.float32) * keep
            h_ref[t, :, :, j * BLK:(j + 1) * BLK] = (
                tile.astype(jnp.bfloat16).reshape(2, ROWS, BLK))
    pl.semaphore_wait(barrier, len(friends))

    names = list(messages())
    index = {n: i for i, n in enumerate(names)}

    def block(s, dy, dz, color):
        zz = (z + dz) % 8
        tile, first, count, y_first = CHUNKS[s]
        rows = pl.ds(first, y_first) if color == "a" else pl.ds(first + y_first, count - y_first)
        return a_buf.at[tile, (y + dy) % 4, zz // 4, zz % 4, rows]

    def block4(s, dz):
        zz = (z + dz) % 8
        tile, first, _, y_first = CHUNKS[s]
        return a_buf.at[tile, :, zz // 4, zz % 4, pl.ds(first, y_first)]

    def lanes(core):
        return pl.ds(pl.multiple_of(core * WIDE, 128), WIDE)

    def b_slot(dx, rb, core):
        return b_buf.at[(x + dx) % 4, rb, :, core]

    def f_slot(dx, s, core, rbs, g):
        tile, first, count, _ = CHUNKS[s]
        return f_buf.at[(x + dx) % 4, rbs, tile, core, pl.ds(first, count), pl.ds(*LANES[g])]

    FULL, LOW, HIGH = pl.ds(0, 4), pl.ds(0, 2), pl.ds(2, 2)
    PAIR = (LOW, HIGH, FULL)

    def ends(name):
        kind = name[0]
        if kind == "Hm":
            s = name[1]
            return (h_ref.at[s, 1 - c], a_buf.at[s, y, zh, zl, :, lanes(c)],
                    a_buf.at[s, y, zh, zl, :, lanes(1 - c)], dev(core=1 - c))
        if kind == "bz+":
            _, s, t = name
            src = block(s, 0, 1 - t, "b")
            return src, src, block(s, 0, -t, "b"), dev(dz=1)
        if kind == "bz-":
            _, s, t = name
            src = block(s, 0, t - 1, "b")
            return src, src, block(s, 0, t, "b"), dev(dz=-1)
        if kind == "by+":
            _, s, dz = name
            src = block(s, 0, dz, "b")
            return src, src, block(s, -1, dz, "b"), dev(dy=1)
        if kind == "by-":
            _, s, dz = name
            src = block(s, 0, dz, "b")
            return src, src, block(s, 1, dz, "b"), dev(dy=-1)
        if kind == "by2":
            _, s, dz = name
            way = 1 if antipode_plus(dz) else -1
            src = block(s, -way, dz, "b")
            return src, src, block(s, 2, dz, "b"), dev(dy=way)
        if kind == "ay+":
            src = block(name[1], 0, 0, "a")
            return src, src, block(name[1], -1, 0, "a"), dev(dy=1)
        if kind == "ay-":
            src = block(name[1], 0, 0, "a")
            return src, src, block(name[1], 1, 0, "a"), dev(dy=-1)
        if kind == "ay2":
            way = 1 if name[1] % 2 == 0 else -1
            src = block(name[1], -way, 0, "a")
            return src, src, block(name[1], 2, 0, "a"), dev(dy=way)
        if kind == "az+":
            _, s, t = name
            src = block4(s, 1 - t)
            return src, src, block4(s, -t), dev(dz=1)
        if kind == "az-":
            _, s, t = name
            src = block4(s, t - 1)
            return src, src, block4(s, t), dev(dz=-1)
        if kind == "Px+":
            src = b_slot(0, name[1], c)
            return src, src, b_slot(-1, name[1], c), dev(dx=1)
        if kind == "Px-":
            src = b_slot(0, name[1], c)
            return src, src, b_slot(1, name[1], c), dev(dx=-1)
        if kind == "Px2":
            way = 1 if name[1] < 2 else -1
            src = b_slot(-way, name[1], c)
            return src, src, b_slot(2, name[1], c), dev(dx=way)
        if kind == "Pm":
            _, dx, rb = name
            src = b_slot(dx, rb, c)
            return src, src, b_slot(dx, rb, 1 - c), dev(core=1 - c)
        if kind in ("Fx+", "Fx-", "F2+", "F2-"):
            _, s, e, g = name
            way = 1 if kind[2] == "+" else -1
            frm, to = (0, -way) if kind[1] == "x" else (-way, 2)
            src = f_slot(frm, s, c, PAIR[e], g)
            return src, src, f_slot(to, s, c, PAIR[e], g), dev(dx=way)
        if kind == "Fm":
            _, dx, s, e, g = name
            src = f_slot(dx, s, c, PAIR[e], g)
            return src, src, f_slot(dx, s, 1 - c, PAIR[e], g), dev(core=1 - c)
        if kind == "Dm":
            return part.at[:, 1 - c], d_mate, d_mate, dev(core=1 - c)
        if kind == "Dr":
            j = name[1]
            return d_chip.at[(y + j) % 4], d_got.at[j - 1], d_got.at[j - 1], dev(dy=j)
        if kind == "Dz":
            k = name[1]
            zz = (z - k) % 8
            src = d_line.at[zh, zl]
            return src, src, d_line.at[zz // 4, zz % 4], dev(dz=k)
        if kind == "Dy":
            j = name[1]
            src = d_all.at[:, y]
            return src, src, d_all.at[:, (y - j) % 4], dev(dy=j)
        raise KeyError(name)

    def outgoing(name):
        src, dst, _, target = ends(name)
        i = index[name]
        return pltpu.make_async_remote_copy(
            src_ref=src, dst_ref=dst, send_sem=send_sem.at[i], recv_sem=recv_sem.at[i],
            device_id=target, device_id_type=MESH)

    def incoming(name):
        src, _, land, target = ends(name)
        i = index[name]
        return pltpu.make_async_remote_copy(
            src_ref=land, dst_ref=land, send_sem=send_sem.at[i], recv_sem=recv_sem.at[i],
            device_id=target, device_id_type=MESH)

    to_side = [row < 15, row > 0, col < 15, col > 0]
    from_side = [row > 0, row < 15, col > 0, col < 15]

    def halo_copy(i):
        return pltpu.make_async_remote_copy(
            src_ref=pot_ref, dst_ref=halo.at[i], send_sem=halo_send.at[i],
            recv_sem=halo_sem.at[i], device_id=beside[i], device_id_type=MESH)

    pot_copy.wait()
    for i in range(4):
        @pl.when(to_side[i])
        def _():
            halo_copy(i).start()

    def wait_halo():
        for i in range(4):
            @pl.when(from_side[i])
            def _():
                halo_copy(i).wait_recv()

            @pl.when(jnp.logical_not(from_side[i]))
            def _():
                halo[i] = jnp.zeros((2, 4, 512), jnp.float32)

    own = [pltpu.make_async_copy(h_ref.at[s, c], a_buf.at[s, y, zh, zl, :, lanes(c)],
                                 local_sem.at[s]) for s in range(STEPS)]
    for copy in own:
        copy.start()

    def p_copy(hf, r):
        q = 2 * c + hf
        src = p_ref.at[hf, :, r]
        here = (q == zl) & (r == c)
        dst = b_buf.at[x, zl, :, r]

        def local():
            return pltpu.make_async_copy(src, dst, pin_sem.at[zl])

        def remote():
            return pltpu.make_async_remote_copy(
                src_ref=src, dst_ref=dst, send_sem=pin_send.at[hf, r], recv_sem=pin_sem.at[zl],
                device_id=dev_line(q, r), device_id_type=MESH)

        return here, local, remote

    def pack_p():
        den_copy.wait()
        lane = lax.broadcasted_iota(jnp.int32, (BLK, BLK), 1)

        def put(hf, t, j, value):
            p_ref[hf, t, :, :, j * BLK:(j + 1) * BLK] = (
                value.astype(jnp.bfloat16).reshape(2, ROWS, BLK))

        for t in range(3):
            tiles = []
            for j in range(3):
                keep = pmask_ref[row * 3 + t, col * 3 + j].astype(jnp.float32)
                tiles.append([
                    den_ref[p, t * BLK:(t + 1) * BLK, j * BLK:(j + 1) * BLK].astype(jnp.float32)
                    * keep for p in range(2)])
            for j in range(2):
                for p in range(2):
                    put(j, t, p, tiles[j][p])
            turned = [pltpu.roll(v, BLK // 2, 1) for v in tiles[2]]
            put(0, t, 2, jnp.where(lane < BLK // 2, tiles[2][0], turned[1]))
            put(1, t, 2, jnp.where(lane < BLK // 2, turned[0], tiles[2][1]))

    def start_p():
        for hf in range(2):
            for r in range(2):
                here, local, remote = p_copy(hf, r)

                @pl.when(here)
                def _():
                    local().start()

                @pl.when(jnp.logical_not(here))
                def _():
                    remote().start()

    def first_product(s, far):
        tile, first, count, _ = CHUNKS[s]
        rows = slice(first, first + count)
        if not far:
            f_acc[tile, :, rows] = jnp.zeros((4, count, WIDE), jnp.float32)

        def body(k, carry):
            yy, zz = (y + (k // 2) + 3) % 4, k % 2
            left = a_buf[tile, yy, zz, :, rows].reshape(4 * count, 2 * WIDE)
            right = b_buf[yy, pl.ds(zz * 2, 2)].reshape(2 * WIDE, WIDE)
            more = jnp.dot(left, right, preferred_element_type=jnp.float32)
            f_acc[tile, :, rows] += more.reshape(4, count, WIDE)
            return carry

        lax.fori_loop(6 if far else 0, 8 if far else 6, body, 0)

    def diagonal(rb, s):
        return d_all[rb].astype(jnp.float32).reshape(STEPS, ROWS, BLK)[s].astype(jnp.bfloat16)

    def first_finish(s):
        tile, first, count, _ = CHUNKS[s]
        rows = slice(first, first + count)
        for rb in range(4):
            right = b_buf[x, rb, tile].reshape(BLK, WIDE)
            total = f_acc[tile, rb, rows] + jnp.dot(diagonal(rb, tile)[rows], right,
                                                    preferred_element_type=jnp.float32)
            f_acc[tile, rb, rows] = total
            f_buf[x, rb, tile, c, rows] = total.astype(jnp.bfloat16)

    def second_product(s, dx, low, high, g):
        lane = slice(LANES[g][0], sum(LANES[g]))
        cuts = [slice(e * WIDE + s * BLK, e * WIDE + (s + 1) * BLK) for e in range(2)]

        def body(k, carry):
            xx, t = (x + (k // (high - low) if dx == 9 else dx)) % 4, low + k % (high - low)
            left = jnp.concatenate(
                [a_buf[t, xx, zz, :, :, cut].reshape(4 * ROWS, BLK)
                 for zz in range(2) for cut in cuts], axis=1)
            right = f_buf[xx, :, s, :, :, lane].reshape(4 * BLK, LANES[g][1])
            more = jnp.dot(left, right, preferred_element_type=jnp.float32)
            s_acc[t, :, :, lane] += more.reshape(4, ROWS, LANES[g][1])
            return carry

        lax.fori_loop(0, (4 if dx == 9 else 1) * (high - low), body, 0)
        if dx in (0, 9) and low <= s < high:
            for rb in range(4):
                right = f_buf[x, rb, s, :, :, lane].reshape(BLK, LANES[g][1])
                s_acc[s, rb, :, lane] += jnp.dot(diagonal(rb, s), right,
                                                 preferred_element_type=jnp.float32)

    def screen():
        wait_halo()
        zero = jnp.zeros((1, 1), jnp.float32)
        for i in range(2):
            for j in range(4):
                here = pot_ref[i, j:j + 1]
                below = pot_ref[0, j:j + 1] if i else halo[0, 1, j:j + 1]
                above = halo[1, 0, j:j + 1] if i else pot_ref[1, j:j + 1]
                left = pot_ref[i, j - 1:j] if j else halo[2, i, 3:4]
                right = pot_ref[i, j + 1:j + 2] if j < 3 else halo[3, i, 0:1]
                later = jnp.concatenate([here[:, 1:], zero], axis=1)
                earlier = jnp.concatenate([zero, here[:, :-1]], axis=1)
                total = above + below
                total = total + right + left
                total = total + later + earlier
                eff[i, j:j + 1] = here + KAPPA * (total - 6.0 * here)

    def integrate(i):
        if i == 0:
            basis_copy.wait()
            part[...] = jnp.zeros_like(part)

        def body(j, carry):
            cell = 2 * i + j
            table = basis_buf[cell // 4, cell % 4]
            scale = eff[cell // 4, pl.ds(cell % 4, 1)]
            weighted = (table.astype(jnp.float32) * scale).astype(jnp.bfloat16)
            for k in range(3):
                rows = slice(k * BLK, (k + 1) * BLK)
                more = lax.dot_general(weighted[rows], table[rows], (((1,), (1,)), ((), ())),
                                       preferred_element_type=jnp.float32)
                part[k] += more.reshape(2, ROWS, BLK)
            return carry

        lax.fori_loop(0, 2, body, 0)

    def line_integrals():
        total = d_chip[y].astype(jnp.float32)
        for j in range(3):
            total = total + d_got[j].astype(jnp.float32)
        d_line[zh, zl] = total.astype(jnp.bfloat16)

    def finish_integrals():
        factor = float(BLK * 2 * 64 * 512) ** -0.5
        total = d_line[0].astype(jnp.float32) + d_line[1].astype(jnp.float32)
        d_all[:, y] = (total * factor).astype(jnp.bfloat16)

    lane_of = lax.broadcasted_iota(jnp.int32, (ROWS, BLK), 1)
    quarter = 0.5 * TIME_STEP * TIME_STEP
    targets = [(zl // 2) * 2 + 1 - zl % 2, 3 - zl, (zl + 2) % 4, zl]

    home = y * 4 + zh * 2 + zl // 2

    def landing(hf, r, j):
        if j == 2:
            return third.at[hf, :, r]
        return out_ref.at[j, :, r, :, pl.ds(pl.multiple_of(hf * BLK, BLK), BLK)]

    def back(k, j):
        src = o_buf.at[k, :, :, pl.ds(j * BLK, BLK)]
        dst = landing(zl % 2, c, j)

        def local():
            return pltpu.make_async_copy(src, dst, ret_sem.at[zl % 2, c, j])

        def remote():
            return pltpu.make_async_remote_copy(
                src_ref=src, dst_ref=dst, send_sem=ret_send.at[k, j],
                recv_sem=ret_sem.at[zl % 2, c, j],
                device_id=dev_line(targets[k], zl // 2), device_id_type=MESH)

        return zl // 2 == c, local, remote

    def get_back(j):
        for hf in range(2):
            for r in range(2):
                land = landing(hf, r, j)
                pltpu.make_async_copy(land, land, ret_sem.at[hf, r, j]).wait()

    def unpack_third():
        lane = lax.broadcasted_iota(jnp.int32, (STEPS * 2 * ROWS, BLK), 1)
        both = [third[hf].astype(jnp.float32).reshape(STEPS * 2 * ROWS, BLK) for hf in range(2)]
        turned = [pltpu.roll(v, BLK // 2, 1) for v in both]
        shape = (STEPS, 2, ROWS, BLK)
        third[0] = jnp.where(lane < BLK // 2, both[0], turned[1]).astype(jnp.bfloat16).reshape(shape)
        third[1] = jnp.where(lane < BLK // 2, turned[0], both[1]).astype(jnp.bfloat16).reshape(shape)

    def third_copy(p):
        return pltpu.make_async_copy(
            third.at[p], out_ref.at[p, :, :, :, pl.ds(2 * BLK, BLK)], third_sem.at[p])

    def give_back(g):
        for k in (1, 2, 0, 3):
            rb = targets[k]
            for s in range(STEPS):
                keep = pmask_ref[(x * 4 + rb) * 3 + s, home * 3 + (2 if g else zl % 2)]
                f = f_acc[s, rb]
                if g:
                    turned = pltpu.roll(f[:, 2 * BLK:], BLK // 2, 1)
                    turn = jnp.where(lane_of < BLK // 2, turned, -turned)
                else:
                    turn = jnp.concatenate([f[:, BLK:2 * BLK], -f[:, :BLK]], axis=1)
                cut = slice(LANES[g][0], sum(LANES[g]))
                base = b_buf[x, rb, s, c, :, cut].astype(jnp.float32)
                o_buf[k, s, :, cut] = (
                    (base + TIME_STEP * turn - quarter * s_acc[s, rb, :, cut])
                    * keep.astype(jnp.float32)).astype(jnp.bfloat16)
            for j in (2,) if g else (0, 1):
                here, local, remote = back(k, j)
                if k < 3:
                    remote().start()
                    continue

                @pl.when(here)
                def _():
                    local().start()

                @pl.when(jnp.logical_not(here))
                def _():
                    remote().start()

    def run(name):
        kind = name[0]
        if kind == "Hready":
            own[name[1]].wait()
        elif kind == "E":
            screen()
        elif kind == "I":
            integrate(name[1])
        elif kind == "C1":
            first_product(name[1], name[2])
        elif kind == "Ff":
            first_finish(name[1])
        elif kind == "S":
            second_product(*name[1:])
        elif kind == "R":
            give_back(name[1])
        elif kind == "Dc":
            d_chip[...] = (part[:, c] + d_mate[...]).reshape(4, 48, BLK).astype(jnp.bfloat16)
        elif kind == "Dl":
            line_integrals()
        elif kind == "Df":
            finish_integrals()

    opened = False
    for what, name in order:
        if what != "send" and not opened:
            opened = True
            pack_p()
            start_p()
            s_acc[...] = jnp.zeros_like(s_acc)
        if what == "send":
            outgoing(name).start()
        elif what == "wait":
            if name[0] == "halo":
                continue
            if name[0] == "P0":
                rb = name[1]
                land = b_buf.at[x, rb, :, c]
                pltpu.make_async_copy(land, land, pin_sem.at[rb]).wait()
            else:
                incoming(name).wait_recv()
        else:
            run(name)

    get_back(2)
    unpack_third()
    for p in range(2):
        third_copy(p).start()
    for what, name in order:
        if what == "send":
            outgoing(name).wait_send()
    for hf in range(2):
        for r in range(2):
            here, _, remote = p_copy(hf, r)

            @pl.when(jnp.logical_not(here))
            def _():
                remote().wait_send()
    get_back(0)
    get_back(1)
    for p in range(2):
        third_copy(p).wait()
    for g in range(3):
        for k in range(3):
            back(k, g)[2]().wait_send()
        here, _, remote = back(3, g)

        @pl.when(jnp.logical_not(here))
        def _():
            remote().wait_send()
    for i in range(4):
        @pl.when(to_side[i])
        def _():
            halo_copy(i).wait_send()


def propagate(h, p, potential, basis, hmask, pmask):
    order, _ = schedule()
    total = len(messages())
    bf, f32 = jnp.bfloat16, jnp.float32
    any_space = pl.BlockSpec(memory_space=pl.ANY)
    smem = pl.BlockSpec(memory_space=pltpu.SMEM)
    return pl.pallas_call(
        functools.partial(core_kernel, order),
        out_shape=jax.ShapeDtypeStruct((2, STEPS, 2, ROWS, WIDE), bf),
        in_specs=[any_space, any_space, any_space, any_space, smem, smem],
        out_specs=any_space,
        scratch_shapes=[
            pltpu.VMEM((STEPS, 4, 2, 4, ROWS, 2 * WIDE), bf),
            pltpu.VMEM((4, 4, STEPS, 2, ROWS, WIDE), bf),
            pltpu.VMEM((4, 4, STEPS, 2, ROWS, WIDE), bf),
            pltpu.VMEM((4, STEPS, ROWS, WIDE), bf),
            pltpu.VMEM((STEPS, 4, ROWS, WIDE), f32),
            pltpu.VMEM((STEPS, 4, ROWS, WIDE), f32),
            pltpu.VMEM((STEPS, ROWS, BLK), f32),
            pltpu.VMEM((4, 48, BLK), bf),
            pltpu.VMEM((4, 4, 48, BLK), bf),
            pltpu.VMEM((3, 48, BLK), bf),
            pltpu.VMEM((2, 4, 48, BLK), bf),
            pltpu.VMEM((2, 4, WIDE, 512), bf),
            pltpu.VMEM((4, 2, 4, 512), f32),
            pltpu.VMEM((2, 4, 512), f32),
            pltpu.VMEM((STEPS, 2, ROWS, BLK), f32),
            pltpu.VMEM((STEPS, 2, ROWS, WIDE), bf),
            pltpu.VMEM((2, STEPS, 2, ROWS, WIDE), bf),
            pltpu.VMEM((WIDE, WIDE), bf),
            pltpu.VMEM((2, WIDE, WIDE), bf),
            pltpu.VMEM((2, 4, 512), f32),
            pltpu.VMEM((2, STEPS, 2, ROWS, BLK), bf),
            pltpu.SemaphoreType.DMA((total,)),
            pltpu.SemaphoreType.DMA((total,)),
            pltpu.SemaphoreType.DMA((STEPS,)),
            pltpu.SemaphoreType.DMA((4,)),
            pltpu.SemaphoreType.DMA((2, 2)),
            pltpu.SemaphoreType.DMA((2, 2, 3)),
            pltpu.SemaphoreType.DMA((4, 3)),
            pltpu.SemaphoreType.DMA((4,)),
            pltpu.SemaphoreType.DMA((4,)),
            pltpu.SemaphoreType.DMA,
            pltpu.SemaphoreType.DMA((3,)),
            pltpu.SemaphoreType.DMA((2,)),
        ],
        compiler_params=pltpu.CompilerParams(
            collective_id=0, has_side_effects=True, vmem_limit_bytes=60 << 20),
        name="propagate",
    )(h, p, potential, basis, hmask, pmask)


def shards(potential, basis, hamiltonian, density, hmask, pmask):
    result = propagate(hamiltonian, density, potential, basis, hmask, pmask)
    return result.reshape(2, WIDE, WIDE)


def solution(mesh):
    in_specs = (
        P("row", "col", None),
        P("row", "col", None, None),
        P("row", "col"),
        P(None, "row", "col"),
        P(),
        P(),
    )
    out_specs = P(None, "row", "col")
    return jax.shard_map(shards, mesh=mesh, in_specs=in_specs, out_specs=out_specs, check_vma=False)
```
